128 devices in a mesh: user: 8 (over y, core), pool: 16 (over x, z).
Axes of the slice: x: 4, y: 4, z: 4, core: 2. Of those that a mesh axis runs over, the one named last changes fastest.
Arguments:
- item_feats: bfloat16 [65536, 512], P(('user', 'pool')), may hold values from -6 to 6
- w_in: bfloat16 [512, 2048], replicated, may hold values from -0.25 to 0.25
- bias_in: float32 [2048], replicated, may hold values from -3 to 3
- w_out: bfloat16 [2048, 512], replicated, may hold values from -0.125 to 0.125
- bilinear: bfloat16 [512, 512], replicated, may hold values from -0.25 to 0.25
- fetch_table: int32 [128, 128, 16], P(None, ('user', 'pool')), may hold values from 0 to 511, as said below
- hist_index: int32 [4096, 256], P(('user', 'pool')), may hold values from 0 to 2047
- hist_len: int32 [4096], P(('user', 'pool')), may hold values from 32 to 256
- route_init: float32 [4096, 4, 256], P(('user', 'pool')), may hold values from -6 to 6
- label_index: int32 [4096], P(('user', 'pool')), may hold values from 0 to 2047
- label_ids: int32 [4096], P(('user', 'pool')), may hold values from 0 to 1048575
- label_counts: int32 [4096], P(('user', 'pool')), may hold values from 1 to 15
- neg_feats: bfloat16 [16384, 512], P(('user', 'pool')), may hold values from -6 to 6
- neg_ids: int32 [16384], P(('user', 'pool')), may hold values from 0 to 1048575
- neg_counts: int32 [16384], P(('user', 'pool')), may hold values from 1 to 15
Outputs:
- interests: float32 [4096, 2048], P(('user', 'pool'))
- user_loss: float32 [4096], P(('user', 'pool'))
The draws below stay inside these ranges and needn't reach their ends.
Inputs may be any that keep to these rules, and one draw needn't show every extreme that they name: fetch_table[b, s, :] names 16 different rows of item block s.
All inputs are finite; a program needn't handle non-finite values.
Results may differ from the reference program's by a relative error of at most 0.0011.
Values may be sent and summed in bfloat16 or wider, within the bound.
A program may use at most 192 MiB of HBM per device.

```python
import math
import jax
import jax.numpy as jnp
import numpy as np
from jax import lax

D = 512
FF = 2048
INTERESTS = 4
HIST = 256
ITERS = 3
VOCAB = 1048576
ITEMS_DEV = 512
CAP = 16
USERS_DEV = 32
ITEMS = 65536
USERS = 4096
NEG = 16384
SLOTS = 2048
DEVICES = 128


def spread_counts(seed_key, shape):
    power_key, rest_key = jax.random.split(seed_key)
    exponent = jax.random.randint(power_key, shape, 0, 4)
    power_base = jnp.left_shift(jnp.ones(shape, jnp.int32), exponent)
    return power_base + jax.random.randint(rest_key, shape, 0, power_base)


def draw_label_counts(key, part):
    return spread_counts(jax.random.fold_in(key, 12), (USERS,)).astype(jnp.int32)


def draw_neg_counts(key, part):
    return spread_counts(jax.random.fold_in(key, 11), (NEG,)).astype(jnp.int32)


def draw_fetch_table(key, part):
    scores = jax.random.randint(jax.random.fold_in(key, 13), (DEVICES, DEVICES, ITEMS_DEV), 0, 262144)
    scores = scores * ITEMS_DEV + lax.broadcasted_iota(jnp.int32, (DEVICES, DEVICES, ITEMS_DEV), 2)
    chosen = lax.top_k(scores, CAP)[1]
    return chosen.astype(jnp.int32)


def place_ends(array, own_key, smallest, largest):
    place = [jax.random.randint(jax.random.fold_in(own_key, axis), (), 0, length) for axis, length in enumerate(array.shape)]
    longest = array.shape.index(max(array.shape))
    beside = place[:longest] + [(place[longest] + 1) % array.shape[longest]] + place[longest + 1:]
    return array.at[tuple(place)].set(smallest).at[tuple(beside)].set(largest)


def levels(own_key, extent, cuts, low, high):
    def one(axis_at, shards_of):
        steps = jax.random.uniform(jax.random.fold_in(jax.random.fold_in(own_key, 6), axis_at), (shards_of,), jnp.float32, low / len(cuts), high / len(cuts))
        return jnp.repeat(jnp.exp(steps), extent[axis_at] // shards_of).reshape((-1,) + (1,) * (len(extent) - axis_at - 1))

    factor_of = one(*cuts[0])
    for cut in cuts[1:]:
        factor_of = factor_of * one(*cut)
    return factor_of


def ranked_wide(own_key, extent, amount, skew):
    loads = [min(1 << octave, amount + 1 - (1 << octave)) * (1 << 20) // math.isqrt((1 << octave) ** skew) + 1 for octave in range((amount + 1).bit_length()) if 1 << octave <= amount]
    width = 1 + sum(loads) // (1 << 30)
    listing = np.cumsum(np.array([max(1, weight // width) for weight in loads]))
    lot = jax.random.randint(jax.random.fold_in(own_key, 1), extent, 0, int(listing[len(loads) - 1]))
    start = jnp.left_shift(1, jnp.searchsorted(jnp.asarray(listing, jnp.int32), lot, side="right").astype(jnp.int32))
    rank = start - 1 + jax.random.randint(jax.random.fold_in(own_key, 4), extent, 0, 1 << 30) % jnp.minimum(start, amount + 1 - start)
    return jax.random.permutation(jax.random.fold_in(own_key, 2), amount)[rank].astype(jnp.int32)


def centred(key, dims, width, limit, cuts=(), kind=jnp.bfloat16):
    values = width * jax.random.normal(key, dims, jnp.float32)
    if cuts:
        values = values * levels(key, dims, cuts, -0.22, 0.18)
    return jnp.clip(values, -limit, limit).astype(kind)


def setup_inputs(seed: int = 0) -> dict:
    arg_keys = jax.random.split(jax.random.key(seed), 16)
    return {
        "item_feats": centred(arg_keys[0], (ITEMS, D), 1.0, 6.0, ((0, 128),)),
        "w_in": centred(arg_keys[1], (D, FF), D ** -0.5, 0.25),
        "bias_in": centred(arg_keys[2], (FF,), 0.5, 3.0, (), jnp.float32),
        "w_out": centred(arg_keys[3], (FF, D), FF ** -0.5, 0.125),
        "bilinear": centred(arg_keys[4], (D, D), D ** -0.5, 0.25),
        "fetch_table": draw_fetch_table(jax.random.fold_in(arg_keys[15], 71), 0),
        "hist_index": place_ends(jax.random.randint(arg_keys[6], (USERS, HIST), 0, SLOTS), jax.random.fold_in(arg_keys[6], 1), 0, SLOTS - 1).astype(jnp.int32),
        "hist_len": place_ends(jax.random.randint(arg_keys[7], (USERS,), HIST // 8, HIST + 1), jax.random.fold_in(arg_keys[7], 1), HIST // 8, HIST).astype(jnp.int32),
        "route_init": centred(arg_keys[8], (USERS, INTERESTS, HIST), 1.0, 6.0, ((0, 128),), jnp.float32),
        "label_index": place_ends(jax.random.randint(arg_keys[9], (USERS,), 0, SLOTS), jax.random.fold_in(arg_keys[9], 1), 0, SLOTS - 1).astype(jnp.int32),
        "label_ids": place_ends(ranked_wide(arg_keys[10], (USERS,), VOCAB, 2), jax.random.fold_in(arg_keys[10], 3), 0, VOCAB - 1).astype(jnp.int32),
        "label_counts": draw_label_counts(jax.random.fold_in(arg_keys[15], 71), 0),
        "neg_feats": centred(arg_keys[12], (NEG, D), 1.0, 6.0, ((0, 128),)),
        "neg_ids": place_ends(ranked_wide(arg_keys[13], (NEG,), VOCAB, 2), jax.random.fold_in(arg_keys[13], 3), 0, VOCAB - 1).astype(jnp.int32),
        "neg_counts": draw_neg_counts(jax.random.fold_in(arg_keys[15], 71), 0),
    }


norm_epsilon = 1e-06
attend_scale = 8.0
logit_scale = 20.0

def item_tower(features, w_in, bias_in, w_out):
    hidden = jnp.dot(features, w_in, preferred_element_type=jnp.float32) + bias_in
    hidden = jnp.maximum(hidden, 0.0).astype(jnp.bfloat16)
    embedding = jnp.dot(hidden, w_out, preferred_element_type=jnp.float32)
    inverse_norm = lax.rsqrt(lax.optimization_barrier(jnp.sum(embedding * embedding, axis=-1, keepdims=True)) + norm_epsilon)
    return (embedding * inverse_norm).astype(jnp.bfloat16)

def dynamic_route(mapped, hist_index, hist_len, route_init):
    history = jnp.take(mapped, hist_index, axis=0).astype(jnp.float32)
    live_mask = (lax.broadcasted_iota(jnp.int32, hist_index.shape, 1) < hist_len[:, None]).astype(jnp.float32)
    route_logits = route_init.astype(jnp.float32)
    capsules = jnp.zeros((hist_index.shape[0], INTERESTS, D), jnp.float32)
    for iteration in range(ITERS):
        raised = jnp.exp(route_logits)
        weights = (raised / lax.optimization_barrier(jnp.sum(raised, axis=1, keepdims=True)) * live_mask[:, None, :]).astype(jnp.bfloat16)
        weights = lax.optimization_barrier(weights).astype(jnp.float32)
        capsule_sums = jnp.einsum('ukl,uld->ukd', weights, history, precision=lax.Precision.HIGHEST)
        norm_sq = lax.optimization_barrier(jnp.sum(capsule_sums * capsule_sums, axis=-1, keepdims=True))
        capsules = capsule_sums * jnp.sqrt(norm_sq) / (1.0 + norm_sq)
        if iteration + 1 < ITERS:
            capsule_half = lax.optimization_barrier(capsules.astype(jnp.bfloat16)).astype(jnp.float32)
            agreement = jnp.einsum('ukd,uld->ukl', capsule_half, history, precision=lax.Precision.HIGHEST)
            route_logits = route_logits + agreement
    return capsules

def label_attention(capsules, label_rows, label_counts):
    scores = attend_scale * lax.optimization_barrier(jnp.sum(capsules * label_rows[:, None, :], axis=-1))
    raised = jnp.exp(scores)
    attention = raised / lax.optimization_barrier(jnp.sum(raised, axis=1, keepdims=True))
    user_vec = lax.optimization_barrier(jnp.sum(attention[:, :, None] * capsules, axis=1)).astype(jnp.bfloat16)
    user_wide = lax.optimization_barrier(user_vec).astype(jnp.float32)
    positive = logit_scale * lax.optimization_barrier(jnp.sum(user_wide * label_rows, axis=-1)) - jnp.log(label_counts.astype(jnp.float32))
    return (user_vec, positive)

def exp_terms(user_vec, label_ids, neg_unit, neg_ids, neg_counts):
    logits = logit_scale * jnp.einsum('ud,nd->un', user_vec.astype(jnp.float32), neg_unit.astype(jnp.float32), precision=lax.Precision.HIGHEST)
    logits = logits - jnp.log(neg_counts.astype(jnp.float32))[None, :]
    keep_mask = neg_ids[None, :] != label_ids[:, None]
    return lax.optimization_barrier(jnp.sum(jnp.where(keep_mask, jnp.exp(logits), 0.0), axis=1))

def reference(item_feats, w_in, bias_in, w_out, bilinear, fetch_table, hist_index, hist_len, route_init, label_index, label_ids, label_counts, neg_feats, neg_ids, neg_counts):
    item_blocks = item_feats.reshape(DEVICES, ITEMS_DEV, D)
    unit = lax.map(lambda block_rows: item_tower(block_rows, w_in, bias_in, w_out), item_blocks)
    neg_unit = item_tower(neg_feats, w_in, bias_in, w_out)

    def per_block(inputs):
        fetch_rows, index_rows, length_rows, init_rows, label_at, label_id, label_count = inputs
        received = jnp.take_along_axis(unit, fetch_rows.astype(jnp.int32)[:, :, None], axis=1).reshape(DEVICES * CAP, D)
        mapped = jnp.dot(received, bilinear, preferred_element_type=jnp.float32).astype(jnp.bfloat16)
        capsules = dynamic_route(mapped, index_rows, length_rows, init_rows)
        label_rows = jnp.take(received, label_at, axis=0).astype(jnp.float32)
        user_vec, positive = label_attention(capsules, label_rows, label_count)
        negative_sum = exp_terms(user_vec, label_id, neg_unit, neg_ids, neg_counts)
        partition = jnp.exp(positive) + negative_sum
        return (capsules.reshape(USERS_DEV, INTERESTS * D), jnp.log(partition) - positive)
    results = lax.map(per_block, (fetch_table, hist_index.reshape(DEVICES, USERS_DEV, HIST), hist_len.reshape(DEVICES, USERS_DEV), route_init.reshape(DEVICES, USERS_DEV, INTERESTS, HIST), label_index.reshape(DEVICES, USERS_DEV), label_ids.reshape(DEVICES, USERS_DEV), label_counts.reshape(DEVICES, USERS_DEV)))
    return (results[0].reshape(USERS, INTERESTS * D), results[1].reshape(USERS))
```

```python
import functools

import jax
import jax.numpy as jnp
from jax import lax
from jax.experimental import pallas as pl
from jax.experimental.pallas import tpu as pltpu
from jax.sharding import PartitionSpec as P

INTERESTS = 4
ITERS = 3
LO = 128

norm_epsilon = 1e-06
attend_scale = 8.0
logit_scale = 20.0

F32 = jnp.float32
BF16 = jnp.bfloat16


def item_tower(features, w_in, bias_in, w_out):
    hidden = jnp.dot(features, w_in, preferred_element_type=F32) + bias_in
    hidden = jnp.maximum(hidden, 0.0).astype(BF16)
    embedding = jnp.dot(hidden, w_out, preferred_element_type=F32)
    inverse_norm = lax.rsqrt(jnp.sum(embedding * embedding, axis=-1, keepdims=True) + norm_epsilon)
    return (embedding * inverse_norm).astype(BF16)


def nt_dot(a, b):
    return lax.dot_general(a, b, (((1,), (1,)), ((), ())), preferred_element_type=F32)


def column(row):
    size = row.shape[1]
    wide = jnp.broadcast_to(row.astype(F32), (size, size))
    eye = lax.broadcasted_iota(jnp.int32, (size, size), 0) == lax.broadcasted_iota(jnp.int32, (size, size), 1)
    return jnp.sum(jnp.where(eye, wide, 0.0), axis=1, keepdims=True)


def prepare_route(index_ref, length_ref, init_ref, low_ref, high_ref, logit_ref):
    users, events = index_ref.shape
    highs = high_ref.shape[1]
    live = lax.broadcasted_iota(jnp.int32, (users, events), 1).astype(F32) < column(length_ref[...])
    marked = jnp.where(live, index_ref[...], -1)
    logit_ref[INTERESTS] = marked.astype(F32)
    for k in range(INTERESTS):
        logit_ref[k] = init_ref[:, k, :]

    def one_user(n, carry):
        row = index_ref[pl.ds(n, 1), :]
        low = jnp.broadcast_to(row & (LO - 1), (LO, events))
        low_ref[n] = jnp.where(low == lax.broadcasted_iota(jnp.int32, (LO, events), 0), 1.0, 0.0).astype(BF16)
        high = jnp.broadcast_to(logit_ref[INTERESTS, pl.ds(n, 1), :], (highs, events))
        first = (lax.broadcasted_iota(jnp.int32, (highs, events), 0) * LO).astype(F32)
        high_ref[n] = jnp.where((high >= first) & (high < first + LO), 1.0, 0.0)
        return carry

    lax.fori_loop(0, users, one_user, 0, unroll=4)


def route(index_ref, mapped_ref, low_ref, high_ref, logit_ref, weight_ref, slot_ref, wide_ref, score_ref):
    users, events = index_ref.shape
    slots = mapped_ref.shape[0]
    highs = slots // LO
    rows = INTERESTS * users
    for iteration in range(ITERS):
        raised = [jnp.exp(logit_ref[k]) for k in range(INTERESTS)]
        total = raised[0] + raised[1] + raised[2] + raised[3]
        for k in range(INTERESTS):
            weight_ref[k] = (raised[k] / total).astype(BF16).astype(F32)

        def one_user(n, carry):
            mask = high_ref[n]
            spread = [
                (jnp.broadcast_to(weight_ref[k, pl.ds(n, 1), :], (highs, events)) * mask).astype(BF16)
                for k in range(INTERESTS)
            ]
            summed = nt_dot(jnp.concatenate(spread, axis=0), low_ref[n])
            for k in range(INTERESTS):
                slot_ref[pl.ds(pl.multiple_of((k * users + n) * highs, highs), highs), :] = summed[
                    k * highs : (k + 1) * highs
                ]
            return carry

        lax.fori_loop(0, users, one_user, 0, unroll=4)
        for high in range(highs):
            part = slot_ref[pl.ds(high, rows, stride=highs), :]
            upper = part.astype(BF16)
            wide_ref[:rows, high * LO : (high + 1) * LO] = upper
            wide_ref[rows:, high * LO : (high + 1) * LO] = (part - upper.astype(F32)).astype(BF16)
        both = jnp.dot(wide_ref[...], mapped_ref[...], preferred_element_type=F32)
        sums = both[:rows] + both[rows:]
        norm_sq = jnp.sum(sums * sums, axis=1, keepdims=True)
        capsules = sums * jnp.sqrt(norm_sq) / (1.0 + norm_sq)
        if iteration + 1 < ITERS:
            score_ref[...] = nt_dot(capsules.astype(BF16), mapped_ref[...])
            for group in range(users // 8):
                for chunk in range(events // LO):
                    at = index_ref[group * 8 : group * 8 + 8, chunk * LO : (chunk + 1) * LO]
                    low = at & (LO - 1)
                    block = at >> 7
                    found = [jnp.zeros((8, LO), F32)] * INTERESTS
                    for high in range(highs):
                        here = block == high
                        for k in range(INTERESTS):
                            scores = score_ref[
                                k * users + group * 8 : k * users + group * 8 + 8, high * LO : (high + 1) * LO
                            ]
                            picked = jnp.take_along_axis(scores, low, axis=1)
                            found[k] = jnp.where(here, picked, found[k])
                    for k in range(INTERESTS):
                        logit_ref[k, group * 8 : group * 8 + 8, chunk * LO : (chunk + 1) * LO] += found[k]
    return capsules


def attend(capsules, received_ref, label_ref, count_ref):
    users = label_ref.shape[1]
    slots = received_ref.shape[0]
    wanted = lax.broadcasted_iota(jnp.int32, (users, slots), 1).astype(F32) == column(label_ref[...])
    label_rows = jnp.dot(
        jnp.where(wanted, 1.0, 0.0).astype(BF16), received_ref[...], preferred_element_type=F32
    )
    each = [capsules[k * users : (k + 1) * users] for k in range(INTERESTS)]
    raised = [jnp.exp(attend_scale * jnp.sum(c * label_rows, axis=1, keepdims=True)) for c in each]
    total = raised[0] + raised[1] + raised[2] + raised[3]
    user_vec = (raised[0] / total) * each[0]
    for k in range(1, INTERESTS):
        user_vec = user_vec + (raised[k] / total) * each[k]
    user_vec = user_vec.astype(BF16)
    positive = logit_scale * jnp.sum(user_vec.astype(F32) * label_rows, axis=1, keepdims=True) - jnp.log(
        column(count_ref[...])
    )
    return user_vec, positive


def route_kernel(
    item_ref, bilinear_ref, index_ref, length_ref, init_ref, label_ref, count_ref,
    interest_ref, vec_ref, positive_ref,
    mapped_ref, low_ref, high_ref, logit_ref, weight_ref, slot_ref, wide_ref, score_ref,
):
    prepare_route(index_ref, length_ref, init_ref, low_ref, high_ref, logit_ref)
    mapped_ref[...] = jnp.dot(item_ref[...], bilinear_ref[...], preferred_element_type=F32).astype(BF16)
    capsules = route(
        index_ref, mapped_ref, low_ref, high_ref, logit_ref, weight_ref, slot_ref, wide_ref, score_ref
    )
    users = index_ref.shape[0]
    width = mapped_ref.shape[1]
    for k in range(INTERESTS):
        interest_ref[:, k * width : (k + 1) * width] = capsules[k * users : (k + 1) * users]
    user_vec, positive = attend(capsules, item_ref, label_ref, count_ref)
    vec_ref[...] = user_vec
    positive_ref[...] = positive


def route_call(received, bilinear, hist_index, hist_len, route_init, label_index, label_counts):
    users, events = hist_index.shape
    slots, width = received.shape
    highs = slots // LO
    rows = INTERESTS * users
    vmem = pl.BlockSpec(memory_space=pltpu.VMEM)
    return pl.pallas_call(
        route_kernel,
        out_shape=(
            jax.ShapeDtypeStruct((users, INTERESTS * width), F32),
            jax.ShapeDtypeStruct((users, width), BF16),
            jax.ShapeDtypeStruct((users, 1), F32),
        ),
        in_specs=[vmem] * 7,
        out_specs=(vmem,) * 3,
        scratch_shapes=[
            pltpu.VMEM((slots, width), BF16),
            pltpu.VMEM((users, LO, events), BF16),
            pltpu.VMEM((users, highs, events), F32),
            pltpu.VMEM((INTERESTS + 1, users, events), F32),
            pltpu.VMEM((INTERESTS, users, events), F32),
            pltpu.VMEM((rows * highs, LO), F32),
            pltpu.VMEM((2 * rows, slots), BF16),
            pltpu.VMEM((rows, slots), F32),
        ],
        compiler_params=pltpu.CompilerParams(vmem_limit_bytes=48 << 20),
    )(
        received, bilinear, hist_index, hist_len.reshape(1, -1), route_init,
        label_index.reshape(1, -1), label_counts.reshape(1, -1),
    )


def exp_terms(user_vec, label_ids, neg_unit, neg_ids, neg_counts):
    logits = logit_scale * jnp.einsum("ud,nd->un", user_vec, neg_unit, preferred_element_type=F32)
    logits = logits - jnp.log(neg_counts.astype(F32))[None, :]
    keep_mask = neg_ids[None, :] != label_ids[:, None]
    return jnp.sum(jnp.where(keep_mask, jnp.exp(logits), 0.0), axis=1)


def on_device(
    item_feats, w_in, bias_in, w_out, bilinear, fetch_table, hist_index, hist_len, route_init,
    label_index, label_ids, label_counts, neg_feats, neg_ids, neg_counts,
):
    unit = item_tower(item_feats, w_in, bias_in, w_out)
    items = unit.shape[0]
    fetch = fetch_table.reshape(-1)
    pick = (fetch[:, None] == lax.broadcasted_iota(jnp.int32, (fetch.shape[0], items), 1)).astype(BF16)
    outgoing = jnp.dot(pick, unit, preferred_element_type=F32).astype(BF16)
    outgoing = outgoing.reshape(fetch_table.shape[0], fetch_table.shape[2], -1)
    received = lax.all_to_all(outgoing, ("user", "pool"), split_axis=0, concat_axis=0, tiled=True)
    received = received.reshape(-1, received.shape[-1])
    interests, user_vec, positive = route_call(
        received, bilinear, hist_index, hist_len, route_init, label_index, label_counts
    )
    positive = positive[:, 0]
    neg_unit = item_tower(neg_feats, w_in, bias_in, w_out)
    pool_unit = lax.all_gather(neg_unit, "pool", axis=0, tiled=True)
    pool_info = lax.all_gather(jnp.stack([neg_ids, neg_counts]), "pool", axis=1, tiled=True)
    vecs = lax.all_gather(user_vec, "user", axis=0, tiled=True)
    labels = lax.all_gather(label_ids, "user", axis=0, tiled=True)
    partial = exp_terms(vecs, labels, pool_unit, pool_info[0], pool_info[1])
    partial = lax.psum_scatter(partial, "user", scatter_dimension=0, tiled=True)
    partition = jnp.exp(positive) + partial
    user_loss = jnp.log(partition) - positive
    return interests, user_loss


def solution(mesh):
    both = ("user", "pool")
    in_specs = (
        P(both, None), P(), P(), P(), P(), P(None, both, None), P(both, None), P(both),
        P(both, None, None), P(both), P(both), P(both), P(both, None), P(both), P(both),
    )
    out_specs = (P(both, None), P(both))
    return jax.shard_map(on_device, mesh=mesh, in_specs=in_specs, out_specs=out_specs, check_vma=False)
```

```python
import functools

import jax
import jax.numpy as jnp
from jax import lax
from jax.experimental import pallas as pl
from jax.experimental.pallas import tpu as pltpu
from jax.sharding import PartitionSpec as P

INTERESTS = 4
ITERS = 3
LO = 128

norm_epsilon = 1e-06
attend_scale = 8.0
logit_scale = 20.0

F32 = jnp.float32
BF16 = jnp.bfloat16


MESH = pl.DeviceIdType.MESH


def item_tower(features, w_in_ref, bias_ref, w_out_ref, hidden_ref):
    rows = features.shape[0]
    hidden = jnp.dot(features, w_in_ref[...], preferred_element_type=F32) + bias_ref[...]
    hidden_ref[:rows] = jnp.maximum(hidden, 0.0).astype(BF16)
    embedding = jnp.dot(hidden_ref[:rows], w_out_ref[...], preferred_element_type=F32)
    inverse_norm = lax.rsqrt(jnp.sum(embedding * embedding, axis=1, keepdims=True) + norm_epsilon)
    return (embedding * inverse_norm).astype(BF16)


def nt_dot(a, b):
    return lax.dot_general(a, b, (((1,), (1,)), ((), ())), preferred_element_type=F32)


def column(row):
    size = row.shape[1]
    wide = jnp.broadcast_to(row.astype(F32), (size, size))
    eye = lax.broadcasted_iota(jnp.int32, (size, size), 0) == lax.broadcasted_iota(jnp.int32, (size, size), 1)
    return jnp.sum(jnp.where(eye, wide, 0.0), axis=1, keepdims=True)


def prepare_route(index_ref, length_ref, init_ref, low_ref, high_ref, logit_ref):
    users, events = index_ref.shape
    highs = high_ref.shape[1]
    live = lax.broadcasted_iota(jnp.int32, (users, events), 1).astype(F32) < column(length_ref[...])
    marked = jnp.where(live, index_ref[...], -1)
    logit_ref[INTERESTS] = marked.astype(F32)
    for k in range(INTERESTS):
        logit_ref[k] = init_ref[:, k, :]

    def one_user(n, carry):
        row = index_ref[pl.ds(n, 1), :]
        low = jnp.broadcast_to(row & (LO - 1), (LO, events))
        low_ref[n] = jnp.where(low == lax.broadcasted_iota(jnp.int32, (LO, events), 0), 1.0, 0.0).astype(BF16)
        high = jnp.broadcast_to(logit_ref[INTERESTS, pl.ds(n, 1), :], (highs, events))
        first = (lax.broadcasted_iota(jnp.int32, (highs, events), 0) * LO).astype(F32)
        high_ref[n] = jnp.where((high >= first) & (high < first + LO), 1.0, 0.0)
        return carry

    lax.fori_loop(0, users, one_user, 0, unroll=4)


def route(index_ref, mapped_ref, low_ref, high_ref, logit_ref, weight_ref, slot_ref, wide_ref, score_ref):
    users, events = index_ref.shape
    slots = mapped_ref.shape[0]
    highs = slots // LO
    rows = INTERESTS * users
    for iteration in range(ITERS):
        raised = [jnp.exp(logit_ref[k]) for k in range(INTERESTS)]
        total = raised[0] + raised[1] + raised[2] + raised[3]
        for k in range(INTERESTS):
            weight_ref[k] = (raised[k] / total).astype(BF16).astype(F32)

        def one_user(n, carry):
            mask = high_ref[n]
            spread = [
                (jnp.broadcast_to(weight_ref[k, pl.ds(n, 1), :], (highs, events)) * mask).astype(BF16)
                for k in range(INTERESTS)
            ]
            summed = nt_dot(jnp.concatenate(spread, axis=0), low_ref[n])
            for k in range(INTERESTS):
                slot_ref[pl.ds(pl.multiple_of((k * users + n) * highs, highs), highs), :] = summed[
                    k * highs : (k + 1) * highs
                ]
            return carry

        lax.fori_loop(0, users, one_user, 0, unroll=4)
        for high in range(highs):
            part = slot_ref[pl.ds(high, rows, stride=highs), :]
            upper = part.astype(BF16)
            wide_ref[:rows, high * LO : (high + 1) * LO] = upper
            wide_ref[rows:, high * LO : (high + 1) * LO] = (part - upper.astype(F32)).astype(BF16)
        both = jnp.dot(wide_ref[...], mapped_ref[...], preferred_element_type=F32)
        sums = both[:rows] + both[rows:]
        norm_sq = jnp.sum(sums * sums, axis=1, keepdims=True)
        capsules = sums * jnp.sqrt(norm_sq) / (1.0 + norm_sq)
        if iteration + 1 < ITERS:
            score_ref[...] = nt_dot(capsules.astype(BF16), mapped_ref[...])
            for group in range(users // 8):
                for chunk in range(events // LO):
                    at = index_ref[group * 8 : group * 8 + 8, chunk * LO : (chunk + 1) * LO]
                    low = at & (LO - 1)
                    block = at >> 7
                    found = [jnp.zeros((8, LO), F32)] * INTERESTS
                    for high in range(highs):
                        here = block == high
                        for k in range(INTERESTS):
                            scores = score_ref[
                                k * users + group * 8 : k * users + group * 8 + 8, high * LO : (high + 1) * LO
                            ]
                            picked = jnp.take_along_axis(scores, low, axis=1)
                            found[k] = jnp.where(here, picked, found[k])
                    for k in range(INTERESTS):
                        logit_ref[k, group * 8 : group * 8 + 8, chunk * LO : (chunk + 1) * LO] += found[k]
    return capsules


def attend(capsules, received_ref, label_ref, count_ref):
    users = label_ref.shape[1]
    slots = received_ref.shape[0]
    wanted = lax.broadcasted_iota(jnp.int32, (users, slots), 1).astype(F32) == column(label_ref[...])
    label_rows = jnp.dot(
        jnp.where(wanted, 1.0, 0.0).astype(BF16), received_ref[...], preferred_element_type=F32
    )
    each = [capsules[k * users : (k + 1) * users] for k in range(INTERESTS)]
    raised = [jnp.exp(attend_scale * jnp.sum(c * label_rows, axis=1, keepdims=True)) for c in each]
    total = raised[0] + raised[1] + raised[2] + raised[3]
    user_vec = (raised[0] / total) * each[0]
    for k in range(1, INTERESTS):
        user_vec = user_vec + (raised[k] / total) * each[k]
    user_vec = user_vec.astype(BF16)
    positive = logit_scale * jnp.sum(user_vec.astype(F32) * label_rows, axis=1, keepdims=True) - jnp.log(
        column(count_ref[...])
    )
    return user_vec, positive


def step_kernel(
    user_count, pool_count,
    feat_ref, w_in_ref, bias_ref, w_out_ref, bilinear_ref, fetch_ref, index_ref, length_ref, init_ref,
    label_ref, label_id_ref, count_ref, neg_feat_ref, neg_id_ref, neg_count_ref,
    interest_ref, loss_ref,
    hidden_ref, unit_ref, outgoing_ref, received_ref, mapped_ref,
    low_ref, high_ref, logit_ref, weight_ref, slot_ref, wide_ref, score_ref,
    neg_ref, info_ref, id_ref, vec_ref, partial_ref, sum_ref,
    item_send, item_recv, item_local, neg_send, neg_recv, info_send, info_recv,
    id_send, id_recv, vec_send, vec_recv, sum_send, sum_recv,
):
    u = lax.axis_index("user")
    p = lax.axis_index("pool")
    me = u * pool_count + p
    devices = user_count * pool_count
    cap = fetch_ref.shape[1]
    users, width = vec_ref.shape[1], vec_ref.shape[2]

    barrier = pltpu.get_barrier_semaphore()

    def greet(step, carry):
        other = (me + step) % devices
        pl.semaphore_signal(
            barrier, inc=1, device_id=(other // pool_count, other % pool_count), device_id_type=MESH
        )
        return carry

    lax.fori_loop(1, devices, greet, 0)

    unit_ref[...] = item_tower(feat_ref[...], w_in_ref, bias_ref, w_out_ref, hidden_ref)
    pl.semaphore_wait(barrier, devices - 1)

    group = pool_count * cap
    items = unit_ref.shape[0]

    def send_items(step, carry):
        to_user = (u + step) % user_count
        fetch = fetch_ref[to_user]
        place = lax.broadcasted_iota(jnp.int32, (cap, items), 1)
        pick = [
            jnp.where(jnp.broadcast_to(fetch[:, at : at + 1], (cap, items)) == place, 1.0, 0.0).astype(BF16)
            for at in range(pool_count)
        ]
        rows = jnp.dot(jnp.concatenate(pick, axis=0), unit_ref[...], preferred_element_type=F32)
        outgoing_ref[pl.ds(pl.multiple_of(to_user * group, group), group), :] = rows.astype(BF16)

        def send(at, carry):
            to_pool = (p + at) % pool_count
            start = pl.multiple_of((to_user * pool_count + to_pool) * cap, cap)
            pltpu.make_async_remote_copy(
                src_ref=outgoing_ref.at[pl.ds(start, cap)],
                dst_ref=received_ref.at[pl.ds(pl.multiple_of(me * cap, cap), cap)],
                send_sem=item_send,
                recv_sem=item_recv.at[u],
                device_id=(to_user, to_pool),
                device_id_type=MESH,
            ).start()
            return carry

        lax.fori_loop(jnp.where(step == 0, 1, 0), pool_count, send, 0)
        return carry

    lax.fori_loop(0, user_count, send_items, 0)
    own = pl.ds(pl.multiple_of(me * cap, cap), cap)
    keep = pltpu.make_async_copy(outgoing_ref.at[own], received_ref.at[own], item_local)
    keep.start()

    id_ref[u] = jnp.broadcast_to(column(label_id_ref[...]), (users, LO))
    info_ref[p] = jnp.concatenate(
        [neg_id_ref[...].astype(F32), jnp.log(neg_count_ref[...].astype(F32)), jnp.zeros((6, LO), F32)], axis=0
    )
    neg_ref[p] = item_tower(neg_feat_ref[...], w_in_ref, bias_ref, w_out_ref, hidden_ref)

    def to_column(ref, send_sem, recv_sem, step):
        to_user = (u + step) % user_count
        return pltpu.make_async_remote_copy(
            src_ref=ref.at[u], dst_ref=ref.at[u], send_sem=send_sem, recv_sem=recv_sem,
            device_id=(to_user, p), device_id_type=MESH,
        )

    def to_row(ref, send_sem, recv_sem, step):
        to_pool = (p + step) % pool_count
        return pltpu.make_async_remote_copy(
            src_ref=ref.at[p], dst_ref=ref.at[p], send_sem=send_sem, recv_sem=recv_sem,
            device_id=(u, to_pool), device_id_type=MESH,
        )

    def send_negatives(step, carry):
        to_row(neg_ref, neg_send, neg_recv, step).start()
        to_row(info_ref, info_send, info_recv, step).start()
        return carry

    lax.fori_loop(1, pool_count, send_negatives, 0)

    def send_ids(step, carry):
        to_column(id_ref, id_send, id_recv, step).start()
        return carry

    lax.fori_loop(1, user_count, send_ids, 0)

    prepare_route(index_ref, length_ref, init_ref, low_ref, high_ref, logit_ref)

    def wait_recv(ref, sem):
        pltpu.make_async_remote_copy(
            src_ref=ref, dst_ref=ref, send_sem=sem, recv_sem=sem, device_id=(u, p), device_id_type=MESH
        ).wait_recv()

    def wait_send(ref, sem):
        pltpu.make_async_remote_copy(
            src_ref=ref, dst_ref=ref, send_sem=sem, recv_sem=sem, device_id=(u, p), device_id_type=MESH
        ).wait_send()

    def map_group(from_user):
        rows = pl.ds(pl.multiple_of(from_user * group, group), group)
        mapped_ref[rows, :] = jnp.dot(
            received_ref[rows, :], bilinear_ref[...], preferred_element_type=F32
        ).astype(BF16)

    keep.wait()
    wait_recv(received_ref.at[pl.ds(0, group - cap)], item_recv.at[u])
    map_group(u)

    def take(step, carry):
        from_user = (u + step) % user_count
        rows = pl.ds(pl.multiple_of(from_user * group, group), group)
        wait_recv(received_ref.at[rows], item_recv.at[from_user])
        map_group(from_user)
        return carry

    lax.fori_loop(1, user_count, take, 0)

    capsules = route(
        index_ref, mapped_ref, low_ref, high_ref, logit_ref, weight_ref, slot_ref, wide_ref, score_ref
    )
    for k in range(INTERESTS):
        interest_ref[:, k * width : (k + 1) * width] = capsules[k * users : (k + 1) * users]
    user_vec, positive = attend(capsules, received_ref, label_ref, count_ref)
    vec_ref[u] = user_vec

    def send_vec(step, carry):
        to_column(vec_ref, vec_send, vec_recv, step).start()
        return carry

    lax.fori_loop(1, user_count, send_vec, 0)
    wait_recv(info_ref.at[pl.ds(0, pool_count - 1)], info_recv)
    wait_recv(id_ref.at[pl.ds(0, user_count - 1)], id_recv)
    wait_recv(neg_ref.at[pl.ds(0, pool_count - 1)], neg_recv)
    wait_recv(vec_ref.at[pl.ds(0, user_count - 1)], vec_recv)

    everyone = user_count * users
    vecs = vec_ref[...].reshape(everyone, width)
    label_ids = id_ref[...].reshape(everyone, LO)

    def one_block(block, total):
        logits = logit_scale * nt_dot(vecs, neg_ref[block]) - info_ref[block, 1:2, :]
        return total + jnp.where(info_ref[block, 0:1, :] != label_ids, jnp.exp(logits), 0.0)

    total = lax.fori_loop(0, pool_count, one_block, jnp.zeros((everyone, LO), F32))
    total = jnp.broadcast_to(jnp.sum(total, axis=1, keepdims=True), (everyone, LO))
    partial_ref[...] = total.reshape(user_count, users, LO)
    sum_ref[u] = partial_ref[u]

    def send_sum(step, carry):
        to_user = (u + step) % user_count
        pltpu.make_async_remote_copy(
            src_ref=partial_ref.at[to_user], dst_ref=sum_ref.at[u], send_sem=sum_send, recv_sem=sum_recv,
            device_id=(to_user, p), device_id_type=MESH,
        ).start()
        return carry

    lax.fori_loop(1, user_count, send_sum, 0)
    wait_recv(sum_ref.at[pl.ds(0, user_count - 1)], sum_recv)
    negative = sum_ref[0]
    for at in range(1, user_count):
        negative = negative + sum_ref[at]
    loss = jnp.log(jnp.exp(positive) + negative[:, :1]) - positive
    eye = lax.broadcasted_iota(jnp.int32, (users, users), 0) == lax.broadcasted_iota(jnp.int32, (users, users), 1)
    loss_ref[...] = jnp.sum(jnp.where(eye, jnp.broadcast_to(loss, (users, users)), 0.0), axis=0, keepdims=True)

    wait_send(outgoing_ref.at[pl.ds(0, (devices - 1) * cap)], item_send)
    wait_send(neg_ref.at[pl.ds(0, pool_count - 1)], neg_send)
    wait_send(info_ref.at[pl.ds(0, pool_count - 1)], info_send)
    wait_send(id_ref.at[pl.ds(0, user_count - 1)], id_send)
    wait_send(vec_ref.at[pl.ds(0, user_count - 1)], vec_send)
    wait_send(partial_ref.at[pl.ds(0, user_count - 1)], sum_send)


def solution(mesh):
    both = ("user", "pool")
    user_count, pool_count = mesh.shape["user"], mesh.shape["pool"]

    def on_device(
        item_feats, w_in, bias_in, w_out, bilinear, fetch_table, hist_index, hist_len, route_init,
        label_index, label_ids, label_counts, neg_feats, neg_ids, neg_counts,
    ):
        users, events = hist_index.shape
        items, width = item_feats.shape
        hidden = w_in.shape[1]
        devices, _, cap = fetch_table.shape
        slots = devices * cap
        highs = slots // LO
        rows = INTERESTS * users
        negatives = neg_feats.shape[0]
        fetch = fetch_table.reshape(user_count, pool_count, cap).transpose(0, 2, 1)
        vmem = pl.BlockSpec(memory_space=pltpu.VMEM)
        dma = pltpu.SemaphoreType.DMA
        interests, loss = pl.pallas_call(
            functools.partial(step_kernel, user_count, pool_count),
            out_shape=(
                jax.ShapeDtypeStruct((users, INTERESTS * width), F32),
                jax.ShapeDtypeStruct((1, users), F32),
            ),
            in_specs=[vmem] * 15,
            out_specs=(vmem,) * 2,
            scratch_shapes=[
                pltpu.VMEM((items, hidden), BF16),
                pltpu.VMEM((items, width), BF16),
                pltpu.VMEM((slots, width), BF16),
                pltpu.VMEM((slots, width), BF16),
                pltpu.VMEM((slots, width), BF16),
                pltpu.VMEM((users, LO, events), BF16),
                pltpu.VMEM((users, highs, events), F32),
                pltpu.VMEM((INTERESTS + 1, users, events), F32),
                pltpu.VMEM((INTERESTS, users, events), F32),
                pltpu.VMEM((rows * highs, LO), F32),
                pltpu.VMEM((2 * rows, slots), BF16),
                pltpu.VMEM((rows, slots), F32),
                pltpu.VMEM((pool_count, negatives, width), BF16),
                pltpu.VMEM((pool_count, 8, LO), F32),
                pltpu.VMEM((user_count, users, LO), F32),
                pltpu.VMEM((user_count, users, width), BF16),
                pltpu.VMEM((user_count, users, LO), F32),
                pltpu.VMEM((user_count, users, LO), F32),
                dma, dma((user_count,)), dma, dma, dma, dma, dma, dma, dma, dma, dma, dma, dma,
            ],
            compiler_params=pltpu.CompilerParams(
                collective_id=0, has_side_effects=True, vmem_limit_bytes=56 << 20
            ),
        )(
            item_feats, w_in, bias_in.reshape(1, -1), w_out, bilinear, fetch, hist_index, hist_len.reshape(1, -1),
            route_init, label_index.reshape(1, -1), label_ids.reshape(1, -1), label_counts.reshape(1, -1),
            neg_feats, neg_ids.reshape(1, -1), neg_counts.reshape(1, -1),
        )
        return interests, loss.reshape(users)

    in_specs = (
        P(both, None), P(), P(), P(), P(), P(None, both, None), P(both, None), P(both),
        P(both, None, None), P(both), P(both), P(both), P(both, None), P(both), P(both),
    )
    out_specs = (P(both, None), P(both))
    return jax.shard_map(on_device, mesh=mesh, in_specs=in_specs, out_specs=out_specs, check_vma=False)
```

```python
import functools

import jax
import jax.numpy as jnp
from jax import lax
from jax.experimental import pallas as pl
from jax.experimental.pallas import tpu as pltpu
from jax.sharding import PartitionSpec as P

INTERESTS = 4
ITERS = 3
LO = 128

norm_epsilon = 1e-06
attend_scale = 8.0
logit_scale = 20.0

F32 = jnp.float32
BF16 = jnp.bfloat16


MESH = pl.DeviceIdType.MESH


def normalised(embedding):
    inverse_norm = lax.rsqrt(jnp.sum(embedding * embedding, axis=1, keepdims=True) + norm_epsilon)
    return (embedding * inverse_norm).astype(BF16)


def first_layer(features, w_in, bias):
    hidden = jnp.dot(features, w_in, preferred_element_type=F32) + bias
    return jnp.maximum(hidden, 0.0).astype(BF16)


def nt_dot(a, b):
    return lax.dot_general(a, b, (((1,), (1,)), ((), ())), preferred_element_type=F32)


def column(row):
    size = row.shape[1]
    wide = jnp.broadcast_to(row.astype(F32), (size, size))
    eye = lax.broadcasted_iota(jnp.int32, (size, size), 0) == lax.broadcasted_iota(jnp.int32, (size, size), 1)
    return jnp.sum(jnp.where(eye, wide, 0.0), axis=1, keepdims=True)


def prepare_route(place_ref, length_ref, init_ref, low_ref, high_ref, logit_ref):
    users, events = place_ref.shape
    highs = high_ref.shape[1]
    live = lax.broadcasted_iota(jnp.int32, (users, events), 1).astype(F32) < column(length_ref[...])
    logit_ref[INTERESTS] = jnp.where(live, place_ref[...], -1).astype(F32)
    for k in range(INTERESTS):
        logit_ref[k] = init_ref[:, k, :]

    def one_user(n, carry):
        low = jnp.broadcast_to(place_ref[pl.ds(n, 1), :] & (LO - 1), (LO, events))
        low_ref[n] = jnp.where(low == lax.broadcasted_iota(jnp.int32, (LO, events), 0), 1.0, 0.0).astype(BF16)
        high = jnp.broadcast_to(logit_ref[INTERESTS, pl.ds(n, 1), :], (highs, events))
        first = (lax.broadcasted_iota(jnp.int32, (highs, events), 0) * LO).astype(F32)
        high_ref[n] = jnp.where((high >= first) & (high < first + LO), 1.0, 0.0)
        return carry

    lax.fori_loop(0, users, one_user, 0, unroll=4)


def spread_weights(low_ref, high_ref, logit_ref, weight_ref, slot_ref, wide_ref):
    _, users, events = weight_ref.shape
    highs = high_ref.shape[1]
    rows = INTERESTS * users
    raised = [jnp.exp(logit_ref[k]) for k in range(INTERESTS)]
    total = raised[0] + raised[1] + raised[2] + raised[3]
    for k in range(INTERESTS):
        weight_ref[k] = (raised[k] / total).astype(BF16).astype(F32)

    def one_user(n, carry):
        mask = high_ref[n]
        spread = [
            (jnp.broadcast_to(weight_ref[k, pl.ds(n, 1), :], (highs, events)) * mask).astype(BF16)
            for k in range(INTERESTS)
        ]
        summed = nt_dot(jnp.concatenate(spread, axis=0), low_ref[n])
        for k in range(INTERESTS):
            slot_ref[pl.ds(pl.multiple_of((k * users + n) * highs, highs), highs), :] = summed[
                k * highs : (k + 1) * highs
            ]
        return carry

    lax.fori_loop(0, users, one_user, 0, unroll=4)
    for high in range(highs):
        part = slot_ref[pl.ds(high, rows, stride=highs), :]
        upper = part.astype(BF16)
        wide_ref[:rows, high * LO : (high + 1) * LO] = upper
        wide_ref[rows:, high * LO : (high + 1) * LO] = (part - upper.astype(F32)).astype(BF16)


def squash(both):
    rows = both.shape[0] // 2
    sums = both[:rows] + both[rows:]
    norm_sq = jnp.sum(sums * sums, axis=1, keepdims=True)
    return sums * jnp.sqrt(norm_sq) / (1.0 + norm_sq)


def add_agreement(capsules, place_ref, mapped_ref, score_ref, logit_ref):
    users, events = place_ref.shape
    highs = mapped_ref.shape[0] // LO
    score_ref[...] = nt_dot(capsules.astype(BF16), mapped_ref[...])
    for group in range(users // 8):
        for chunk in range(events // LO):
            at = place_ref[group * 8 : group * 8 + 8, chunk * LO : (chunk + 1) * LO]
            low = at & (LO - 1)
            block = at >> 7
            found = [jnp.zeros((8, LO), F32)] * INTERESTS
            for high in range(highs):
                here = block == high
                for k in range(INTERESTS):
                    scores = score_ref[
                        k * users + group * 8 : k * users + group * 8 + 8, high * LO : (high + 1) * LO
                    ]
                    picked = jnp.take_along_axis(scores, low, axis=1)
                    found[k] = jnp.where(here, picked, found[k])
            for k in range(INTERESTS):
                logit_ref[k, group * 8 : group * 8 + 8, chunk * LO : (chunk + 1) * LO] += found[k]


def attend(capsules, received_ref, label_place, count_ref):
    users = label_place.shape[1]
    slots = received_ref.shape[0]
    wanted = lax.broadcasted_iota(jnp.int32, (users, slots), 1).astype(F32) == column(label_place)
    label_rows = jnp.dot(
        jnp.where(wanted, 1.0, 0.0).astype(BF16), received_ref[...], preferred_element_type=F32
    )
    each = [capsules[k * users : (k + 1) * users] for k in range(INTERESTS)]
    raised = [jnp.exp(attend_scale * jnp.sum(c * label_rows, axis=1, keepdims=True)) for c in each]
    total = raised[0] + raised[1] + raised[2] + raised[3]
    user_vec = (raised[0] / total) * each[0]
    for k in range(1, INTERESTS):
        user_vec = user_vec + (raised[k] / total) * each[k]
    user_vec = user_vec.astype(BF16)
    positive = logit_scale * jnp.sum(user_vec.astype(F32) * label_rows, axis=1, keepdims=True) - jnp.log(
        column(count_ref[...])
    )
    return user_vec, positive


def step_kernel(
    user_count, pool_count,
    feat_hbm, w_in_hbm, bias_ref, w_out_hbm, bilinear_hbm, fetch_ref, index_ref, length_ref, init_ref,
    label_ref, label_id_ref, count_ref, neg_feat_ref, neg_id_ref, neg_count_ref,
    interest_ref, loss_ref,
    feat_ref, w_in_ref, w_out_ref, bilinear_ref, pick_ref, hidden_ref, unit_ref, outgoing_ref, received_ref,
    mapped_ref, place_ref, low_ref, high_ref, logit_ref, weight_ref, slot_ref, wide_ref, both_ref, score_ref,
    neg_ref, info_ref, id_ref, vec_ref, partial_ref, sum_ref,
    load_sem, ready_sem, item_send, item_recv, item_local, neg_send, neg_recv, info_send, info_recv,
    id_send, id_recv, vec_send, vec_recv, sum_send, sum_recv,
):
    u = lax.axis_index("user")
    p = lax.axis_index("pool")
    devices = user_count * pool_count
    cap = fetch_ref.shape[0]
    users, width = vec_ref.shape[1], vec_ref.shape[2]
    items = unit_ref.shape[0]
    hidden = w_in_ref.shape[1]
    chunks = 4
    part = hidden // chunks
    spread = LO // users
    lines = pool_count // spread

    loads = [pltpu.make_async_copy(feat_hbm, feat_ref, load_sem.at[0])]
    for at in range(chunks):
        cut = pl.ds(at * part, part)
        loads.append(pltpu.make_async_copy(w_in_hbm.at[:, cut], w_in_ref.at[:, cut], load_sem.at[1 + at]))
    loads.append(pltpu.make_async_copy(w_out_hbm, w_out_ref, load_sem.at[1 + chunks]))
    loads.append(pltpu.make_async_copy(bilinear_hbm, bilinear_ref, load_sem.at[2 + chunks]))
    for load in loads:
        load.start()

    barrier = pltpu.get_barrier_semaphore()
    for step in range(1, pool_count):
        pl.semaphore_signal(barrier, inc=1, device_id=(u, (p + step) % pool_count), device_id_type=MESH)
    for step in range(1, user_count):
        pl.semaphore_signal(barrier, inc=1, device_id=((u + step) % user_count, p), device_id_type=MESH)

    place = lax.broadcasted_iota(jnp.int32, (cap, items), 1)
    for at in range(devices):
        wanted = jnp.broadcast_to(fetch_ref[:, at : at + 1], (cap, items)) == place
        pick_ref[at * cap : (at + 1) * cap, :] = jnp.where(wanted, 1.0, 0.0).astype(BF16)

    loads[0].wait()
    for at in range(chunks):
        loads[1 + at].wait()
        cut = slice(at * part, (at + 1) * part)
        hidden_ref[:, cut] = first_layer(feat_ref[...], w_in_ref[:, cut], bias_ref[:, cut])
    pl.semaphore_wait(barrier, pool_count + user_count - 2)
    for step in range(1, user_count):
        pl.semaphore_signal(ready_sem, inc=1, device_id=((u + step) % user_count, p), device_id_type=MESH)
    loads[1 + chunks].wait()
    unit_ref[...] = normalised(jnp.dot(hidden_ref[...], w_out_ref[...], preferred_element_type=F32))
    group = pool_count * cap
    for at in range(user_count):
        rows = slice(at * group, (at + 1) * group)
        outgoing_ref[rows, :] = jnp.dot(pick_ref[rows, :], unit_ref[...], preferred_element_type=F32).astype(BF16)
    pl.semaphore_wait(ready_sem, user_count - 1)

    def send_round(r, carry):
        def send(j, carry):
            to_user = (u + r + j) % user_count
            to_pool = (p + j) % pool_count
            source = pl.multiple_of((to_user * pool_count + to_pool) * cap, cap)
            target = pl.multiple_of((r * pool_count + j) * cap, cap)
            pltpu.make_async_remote_copy(
                src_ref=outgoing_ref.at[pl.ds(source, cap)],
                dst_ref=received_ref.at[pl.ds(target, cap)],
                send_sem=item_send,
                recv_sem=item_recv.at[r],
                device_id=(to_user, to_pool),
                device_id_type=MESH,
            ).start()
            return carry

        lax.fori_loop(jnp.where(r == 0, 1, 0), pool_count, send, 0)
        return carry

    lax.fori_loop(0, user_count, send_round, 0)
    own = pl.multiple_of((u * pool_count + p) * cap, cap)
    keep = pltpu.make_async_copy(outgoing_ref.at[pl.ds(own, cap)], received_ref.at[pl.ds(0, cap)], item_local)
    keep.start()

    def places(slot):
        from_user = slot // (pool_count * cap)
        from_pool = (slot // cap) % pool_count
        j = (p - from_pool + pool_count) % pool_count
        r = (u - from_user - j + 4 * user_count) % user_count
        return (r * pool_count + j) * cap + slot % cap

    lane = lax.broadcasted_iota(jnp.int32, (1, LO), 1)
    ids = jnp.concatenate([label_id_ref[...].astype(F32)] * spread, axis=1)
    id_ref[p] = jnp.broadcast_to(jnp.where(lane // users == p % spread, ids, 0.0), (8, LO))
    info_ref[u] = jnp.concatenate(
        [neg_id_ref[...].astype(F32), jnp.log(neg_count_ref[...].astype(F32)), jnp.zeros((6, LO), F32)], axis=0
    )
    negatives = neg_feat_ref.shape[0]
    hidden_ref[:negatives] = first_layer(neg_feat_ref[...], w_in_ref[...], bias_ref[...])
    neg_ref[u] = normalised(jnp.dot(hidden_ref[:negatives], w_out_ref[...], preferred_element_type=F32))
    place_ref[...] = places(index_ref[...])
    label_place = places(label_ref[...])
    prepare_route(place_ref, length_ref, init_ref, low_ref, high_ref, logit_ref)
    spread_weights(low_ref, high_ref, logit_ref, weight_ref, slot_ref, wide_ref)

    def along_user(ref, send_sem, recv_sem, step):
        return pltpu.make_async_remote_copy(
            src_ref=ref.at[u], dst_ref=ref.at[u], send_sem=send_sem, recv_sem=recv_sem,
            device_id=((u + step) % user_count, p), device_id_type=MESH,
        )

    def along_pool(ref, send_sem, recv_sem, step):
        return pltpu.make_async_remote_copy(
            src_ref=ref.at[p], dst_ref=ref.at[p], send_sem=send_sem, recv_sem=recv_sem,
            device_id=(u, (p + step) % pool_count), device_id_type=MESH,
        )

    def wait_recv(ref, sem):
        pltpu.make_async_remote_copy(
            src_ref=ref, dst_ref=ref, send_sem=sem, recv_sem=sem, device_id=(u, p), device_id_type=MESH
        ).wait_recv()

    def wait_send(ref, sem):
        pltpu.make_async_remote_copy(
            src_ref=ref, dst_ref=ref, send_sem=sem, recv_sem=sem, device_id=(u, p), device_id_type=MESH
        ).wait_send()

    def take(r):
        cut = pl.ds(pl.multiple_of(r * group, group), group)
        mapped_ref[cut, :] = jnp.dot(
            received_ref[cut, :], bilinear_ref[...], preferred_element_type=F32
        ).astype(BF16)
        return jnp.dot(wide_ref[:, cut], mapped_ref[cut, :], preferred_element_type=F32)

    loads[2 + chunks].wait()
    keep.wait()
    wait_recv(received_ref.at[pl.ds(0, group - cap)], item_recv.at[0])
    both_ref[...] = take(0)

    def take_round(r, carry):
        wait_recv(received_ref.at[pl.ds(pl.multiple_of(r * group, group), group)], item_recv.at[r])
        both_ref[...] += take(r)
        return carry

    lax.fori_loop(1, user_count, take_round, 0)

    def send_negatives(step, carry):
        along_user(neg_ref, neg_send, neg_recv, step).start()
        along_user(info_ref, info_send, info_recv, step).start()
        return carry

    lax.fori_loop(1, user_count, send_negatives, 0)

    def send_ids(step, carry):
        along_pool(id_ref, id_send, id_recv, step).start()
        return carry

    lax.fori_loop(1, pool_count, send_ids, 0)

    capsules = squash(both_ref[...])
    for _ in range(1, ITERS):
        add_agreement(capsules, place_ref, mapped_ref, score_ref, logit_ref)
        spread_weights(low_ref, high_ref, logit_ref, weight_ref, slot_ref, wide_ref)
        capsules = squash(jnp.dot(wide_ref[...], mapped_ref[...], preferred_element_type=F32))
    user_vec, positive = attend(capsules, received_ref, label_place, count_ref)
    vec_ref[p] = user_vec

    def send_vec(step, carry):
        along_pool(vec_ref, vec_send, vec_recv.at[p // spread], step).start()
        return carry

    lax.fori_loop(1, pool_count, send_vec, 0)
    for k in range(INTERESTS):
        interest_ref[:, k * width : (k + 1) * width] = capsules[k * users : (k + 1) * users]
    wait_recv(info_ref.at[pl.ds(0, user_count - 1)], info_recv)
    wait_recv(id_ref.at[pl.ds(0, pool_count - 1)], id_recv)
    wait_recv(neg_ref.at[pl.ds(0, user_count - 1)], neg_recv)
    neg_ids = jnp.concatenate([column(info_ref[at, 0:1, :]) for at in range(user_count)], axis=0)
    neg_logs = jnp.concatenate([column(info_ref[at, 1:2, :]) for at in range(user_count)], axis=0)
    neg_rows = neg_ref[...].reshape(user_count * negatives, width)

    def one_line(line, own_line):
        first = pl.multiple_of(line * spread, spread)
        wait_recv(vec_ref.at[pl.ds(0, spread - 1 if own_line else spread)], vec_recv.at[line])
        vecs = vec_ref[pl.ds(first, spread)].reshape(LO, width)
        line_ids = id_ref[first, 0:1, :]
        for at in range(1, spread):
            line_ids = line_ids + id_ref[first + at, 0:1, :]
        logits = logit_scale * nt_dot(neg_rows, vecs) - neg_logs
        kept = jnp.where(neg_ids != line_ids, jnp.exp(logits), 0.0)
        partial_ref[line] = jnp.broadcast_to(jnp.sum(kept, axis=0, keepdims=True), (8, LO))

    def send_sum(line, to_pool):
        pltpu.make_async_remote_copy(
            src_ref=partial_ref.at[line], dst_ref=sum_ref.at[p], send_sem=sum_send, recv_sem=sum_recv,
            device_id=(u, to_pool), device_id_type=MESH,
        ).start()

    own_line = p // spread
    one_line(own_line, True)
    sum_ref[p] = partial_ref[own_line]

    def send_own(step, carry):
        send_sum(own_line, own_line * spread + (p + step) % spread)
        return carry

    lax.fori_loop(1, spread, send_own, 0)

    def other_line(step, carry):
        line = (own_line + step) % lines
        one_line(line, False)

        def send_other(at, carry):
            send_sum(line, line * spread + (p + at) % spread)
            return carry

        lax.fori_loop(0, spread, send_other, 0)
        return carry

    lax.fori_loop(1, lines, other_line, 0)
    wait_recv(sum_ref.at[pl.ds(0, pool_count - 1)], sum_recv)
    negative = sum_ref[0]
    for at in range(1, pool_count):
        negative = negative + sum_ref[at]
    mine = lax.broadcasted_iota(jnp.int32, (users, LO), 1) == (
        lax.broadcasted_iota(jnp.int32, (users, LO), 0) + (p % spread) * users
    )
    negative = jnp.sum(
        jnp.where(mine, jnp.broadcast_to(negative[0:1], (users, LO)), 0.0), axis=1, keepdims=True
    )
    loss = jnp.log(jnp.exp(positive) + negative) - positive
    eye = lax.broadcasted_iota(jnp.int32, (users, users), 0) == lax.broadcasted_iota(jnp.int32, (users, users), 1)
    loss_ref[...] = jnp.sum(jnp.where(eye, jnp.broadcast_to(loss, (users, users)), 0.0), axis=0, keepdims=True)

    wait_send(outgoing_ref.at[pl.ds(0, (devices - 1) * cap)], item_send)
    wait_send(neg_ref.at[pl.ds(0, user_count - 1)], neg_send)
    wait_send(info_ref.at[pl.ds(0, user_count - 1)], info_send)
    wait_send(id_ref.at[pl.ds(0, pool_count - 1)], id_send)
    wait_send(vec_ref.at[pl.ds(0, pool_count - 1)], vec_send)
    wait_send(sum_ref.at[pl.ds(0, pool_count - 1)], sum_send)


def solution(mesh):
    both = ("user", "pool")
    user_count, pool_count = mesh.shape["user"], mesh.shape["pool"]

    def on_device(
        item_feats, w_in, bias_in, w_out, bilinear, fetch_table, hist_index, hist_len, route_init,
        label_index, label_ids, label_counts, neg_feats, neg_ids, neg_counts,
    ):
        users, events = hist_index.shape
        items, width = item_feats.shape
        hidden = w_in.shape[1]
        devices, _, cap = fetch_table.shape
        slots = devices * cap
        highs = slots // LO
        rows = INTERESTS * users
        negatives = neg_feats.shape[0]
        vmem = pl.BlockSpec(memory_space=pltpu.VMEM)
        hbm = pl.BlockSpec(memory_space=pl.ANY)
        dma = pltpu.SemaphoreType.DMA
        interests, loss = pl.pallas_call(
            functools.partial(step_kernel, user_count, pool_count),
            out_shape=(
                jax.ShapeDtypeStruct((users, INTERESTS * width), F32),
                jax.ShapeDtypeStruct((1, users), F32),
            ),
            in_specs=[hbm, hbm, vmem, hbm, hbm] + [vmem] * 10,
            out_specs=(vmem,) * 2,
            scratch_shapes=[
                pltpu.VMEM((items, width), BF16),
                pltpu.VMEM((width, hidden), BF16),
                pltpu.VMEM((hidden, width), BF16),
                pltpu.VMEM((width, width), BF16),
                pltpu.VMEM((slots, items), BF16),
                pltpu.VMEM((items, hidden), BF16),
                pltpu.VMEM((items, width), BF16),
                pltpu.VMEM((slots, width), BF16),
                pltpu.VMEM((slots, width), BF16),
                pltpu.VMEM((slots, width), BF16),
                pltpu.VMEM((users, events), jnp.int32),
                pltpu.VMEM((users, LO, events), BF16),
                pltpu.VMEM((users, highs, events), F32),
                pltpu.VMEM((INTERESTS + 1, users, events), F32),
                pltpu.VMEM((INTERESTS, users, events), F32),
                pltpu.VMEM((rows * highs, LO), F32),
                pltpu.VMEM((2 * rows, slots), BF16),
                pltpu.VMEM((2 * rows, width), F32),
                pltpu.VMEM((rows, slots), F32),
                pltpu.VMEM((user_count, negatives, width), BF16),
                pltpu.VMEM((user_count, 8, LO), F32),
                pltpu.VMEM((pool_count, 8, LO), F32),
                pltpu.VMEM((pool_count, users, width), BF16),
                pltpu.VMEM((pool_count * users // LO, 8, LO), F32),
                pltpu.VMEM((pool_count, 8, LO), F32),
                dma((7,)), pltpu.SemaphoreType.REGULAR,
                dma, dma((user_count,)), dma, dma, dma, dma, dma, dma, dma,
                dma, dma((pool_count * users // LO,)), dma, dma,
            ],
            compiler_params=pltpu.CompilerParams(
                collective_id=0, has_side_effects=True, vmem_limit_bytes=56 << 20
            ),
        )(
            item_feats, w_in, bias_in.reshape(1, -1), w_out, bilinear, fetch_table[:, 0, :].T, hist_index,
            hist_len.reshape(1, -1), route_init, label_index.reshape(1, -1), label_ids.reshape(1, -1),
            label_counts.reshape(1, -1), neg_feats, neg_ids.reshape(1, -1), neg_counts.reshape(1, -1),
        )
        return interests, loss.reshape(users)

    in_specs = (
        P(both, None), P(), P(), P(), P(), P(None, both, None), P(both, None), P(both),
        P(both, None, None), P(both), P(both), P(both), P(both, None), P(both), P(both),
    )
    out_specs = (P(both, None), P(both))
    return jax.shard_map(on_device, mesh=mesh, in_specs=in_specs, out_specs=out_specs, check_vma=False)
```

```python
import functools

import jax
import jax.numpy as jnp
from jax import lax
from jax.experimental import pallas as pl
from jax.experimental.pallas import tpu as pltpu
from jax.sharding import PartitionSpec as P

INTERESTS = 4
ITERS = 3
LO = 128

norm_epsilon = 1e-06
attend_scale = 8.0
logit_scale = 20.0

F32 = jnp.float32
BF16 = jnp.bfloat16


MESH = pl.DeviceIdType.MESH


HOPS = (0, 1, 2, 1)
FARTHEST = sorted(
    ((dy, dc, dx, dz) for dy in range(4) for dc in range(2) for dx in range(4) for dz in range(4)),
    key=lambda d: (-HOPS[d[0]] - HOPS[d[2]] - HOPS[d[3]], (d[0] + d[2] + d[3]) % 4, -d[1]),
)
TURN = [0] * len(FARTHEST)
for turn, (dy, dc, dx, dz) in enumerate(FARTHEST):
    TURN[((dy * 2 + dc) * 4 + dx) * 4 + dz] = turn


def normalised(embedding):
    inverse_norm = lax.rsqrt(jnp.sum(embedding * embedding, axis=1, keepdims=True) + norm_epsilon)
    return (embedding * inverse_norm).astype(BF16)


def first_layer(features, w_in, bias):
    hidden = jnp.dot(features, w_in, preferred_element_type=F32) + bias
    return jnp.maximum(hidden, 0.0).astype(BF16)


def nt_dot(a, b):
    return lax.dot_general(a, b, (((1,), (1,)), ((), ())), preferred_element_type=F32)


def column(row):
    size = row.shape[1]
    wide = jnp.broadcast_to(row.astype(F32), (size, size))
    eye = lax.broadcasted_iota(jnp.int32, (size, size), 0) == lax.broadcasted_iota(jnp.int32, (size, size), 1)
    return jnp.sum(jnp.where(eye, wide, 0.0), axis=1, keepdims=True)


def prepare_route(place_ref, length_ref, init_ref, low_ref, high_ref, logit_ref):
    users, events = place_ref.shape
    highs = high_ref.shape[1]
    live = lax.broadcasted_iota(jnp.int32, (users, events), 1).astype(F32) < column(length_ref[...])
    logit_ref[INTERESTS] = jnp.where(live, place_ref[...], -1).astype(F32)
    for k in range(INTERESTS):
        logit_ref[k] = init_ref[:, k, :]

    def one_user(n, carry):
        low = jnp.broadcast_to(place_ref[pl.ds(n, 1), :] & (LO - 1), (LO, events))
        low_ref[n] = jnp.where(low == lax.broadcasted_iota(jnp.int32, (LO, events), 0), 1.0, 0.0).astype(BF16)
        high = jnp.broadcast_to(logit_ref[INTERESTS, pl.ds(n, 1), :], (highs, events))
        first = (lax.broadcasted_iota(jnp.int32, (highs, events), 0) * LO).astype(F32)
        high_ref[n] = jnp.where((high >= first) & (high < first + LO), 1.0, 0.0)
        return carry

    lax.fori_loop(0, users, one_user, 0, unroll=4)


def spread_weights(low_ref, high_ref, logit_ref, weight_ref, slot_ref, wide_ref):
    _, users, events = weight_ref.shape
    highs = high_ref.shape[1]
    rows = INTERESTS * users
    raised = [jnp.exp(logit_ref[k]) for k in range(INTERESTS)]
    total = raised[0] + raised[1] + raised[2] + raised[3]
    for k in range(INTERESTS):
        weight_ref[k] = (raised[k] / total).astype(BF16).astype(F32)

    def one_user(n, carry):
        mask = high_ref[n]
        spread = [
            (jnp.broadcast_to(weight_ref[k, pl.ds(n, 1), :], (highs, events)) * mask).astype(BF16)
            for k in range(INTERESTS)
        ]
        summed = nt_dot(jnp.concatenate(spread, axis=0), low_ref[n])
        for k in range(INTERESTS):
            slot_ref[pl.ds(pl.multiple_of((k * users + n) * highs, highs), highs), :] = summed[
                k * highs : (k + 1) * highs
            ]
        return carry

    lax.fori_loop(0, users, one_user, 0, unroll=4)
    for high in range(highs):
        part = slot_ref[pl.ds(high, rows, stride=highs), :]
        upper = part.astype(BF16)
        wide_ref[:rows, high * LO : (high + 1) * LO] = upper
        wide_ref[rows:, high * LO : (high + 1) * LO] = (part - upper.astype(F32)).astype(BF16)


def squash(both):
    rows = both.shape[0] // 2
    sums = both[:rows] + both[rows:]
    norm_sq = jnp.sum(sums * sums, axis=1, keepdims=True)
    return sums * jnp.sqrt(norm_sq) / (1.0 + norm_sq)


def add_agreement(capsules, place_ref, mapped_ref, score_ref, logit_ref):
    users, events = place_ref.shape
    highs = mapped_ref.shape[0] // LO
    score_ref[...] = nt_dot(capsules.astype(BF16), mapped_ref[...])
    for group in range(users // 8):
        for chunk in range(events // LO):
            at = place_ref[group * 8 : group * 8 + 8, chunk * LO : (chunk + 1) * LO]
            low = at & (LO - 1)
            block = at >> 7
            found = [jnp.zeros((8, LO), F32)] * INTERESTS
            for high in range(highs):
                here = block == high
                for k in range(INTERESTS):
                    scores = score_ref[
                        k * users + group * 8 : k * users + group * 8 + 8, high * LO : (high + 1) * LO
                    ]
                    picked = jnp.take_along_axis(scores, low, axis=1)
                    found[k] = jnp.where(here, picked, found[k])
            for k in range(INTERESTS):
                logit_ref[k, group * 8 : group * 8 + 8, chunk * LO : (chunk + 1) * LO] += found[k]


def attend(capsules, received_ref, label_place, count_ref):
    users = label_place.shape[1]
    slots = received_ref.shape[0]
    wanted = lax.broadcasted_iota(jnp.int32, (users, slots), 1).astype(F32) == column(label_place)
    label_rows = jnp.dot(
        jnp.where(wanted, 1.0, 0.0).astype(BF16), received_ref[...], preferred_element_type=F32
    )
    each = [capsules[k * users : (k + 1) * users] for k in range(INTERESTS)]
    raised = [jnp.exp(attend_scale * jnp.sum(c * label_rows, axis=1, keepdims=True)) for c in each]
    total = raised[0] + raised[1] + raised[2] + raised[3]
    user_vec = (raised[0] / total) * each[0]
    for k in range(1, INTERESTS):
        user_vec = user_vec + (raised[k] / total) * each[k]
    user_vec = user_vec.astype(BF16)
    positive = logit_scale * jnp.sum(user_vec.astype(F32) * label_rows, axis=1, keepdims=True) - jnp.log(
        column(count_ref[...])
    )
    return user_vec, positive


def step_kernel(
    user_count, pool_count,
    feat_hbm, w_in_hbm, bias_hbm, w_out_hbm, bilinear_hbm, fetch_hbm, index_hbm, length_hbm, init_hbm,
    label_hbm, label_id_hbm, count_hbm, neg_feat_hbm, neg_id_hbm, neg_count_hbm, turn_hbm,
    result_ref,
    feat_ref, w_in_ref, bias_ref, w_out_ref, bilinear_ref, fetch_ref, index_ref, length_ref, init_ref,
    label_ref, label_id_ref, count_ref, neg_feat_ref, neg_id_ref, neg_count_ref, turn_ref, pick_ref, hidden_ref, unit_ref, outgoing_ref, received_ref,
    mapped_ref, place_ref, low_ref, high_ref, logit_ref, weight_ref, slot_ref, wide_ref, both_ref, score_ref,
    neg_ref, info_ref, id_ref, vec_ref, partial_ref, sum_ref,
    load_sem, item_send, item_recv, item_local, neg_send, neg_recv, info_send, info_recv,
    id_send, id_recv, vec_send, vec_recv, sum_send, sum_recv,
):
    u = lax.axis_index("user")
    p = lax.axis_index("pool")
    devices = user_count * pool_count
    cap = fetch_ref.shape[0]
    users, width = vec_ref.shape[1], vec_ref.shape[2]
    items = unit_ref.shape[0]
    hidden = w_in_ref.shape[1]
    chunks = 4
    part = hidden // chunks
    spread = LO // users
    lines = pool_count // spread

    early = [pltpu.make_async_copy(fetch_hbm, fetch_ref, load_sem.at[0])]
    early.append(pltpu.make_async_copy(feat_hbm, feat_ref, load_sem.at[1]))
    early.append(pltpu.make_async_copy(bias_hbm, bias_ref, load_sem.at[2]))
    for at in range(chunks):
        cut = pl.ds(at * part, part)
        early.append(pltpu.make_async_copy(w_in_hbm.at[:, cut], w_in_ref.at[:, cut], load_sem.at[3 + at]))
    early.append(pltpu.make_async_copy(w_out_hbm, w_out_ref, load_sem.at[3 + chunks]))
    pairs = [
        (neg_feat_hbm, neg_feat_ref), (index_hbm, index_ref), (length_hbm, length_ref), (init_hbm, init_ref),
        (label_hbm, label_ref), (label_id_hbm, label_id_ref), (count_hbm, count_ref), (neg_id_hbm, neg_id_ref),
        (neg_count_hbm, neg_count_ref), (turn_hbm, turn_ref), (bilinear_hbm, bilinear_ref),
    ]
    late = [
        pltpu.make_async_copy(source, target, load_sem.at[4 + chunks + at])
        for at, (source, target) in enumerate(pairs)
    ]
    for load in early + late:
        load.start()

    y, c, x, z = u // 2, u % 2, p // 4, p % 4
    near_y = [((y + d) % 4) * 2 for d in range(4)]
    near_c = [c, 1 - c]
    near_x = [((x + d) % 4) * 4 for d in range(4)]
    near_z = [(z + d) % 4 for d in range(4)]
    partners = [(near_y[dy] + near_c[dc], near_x[dx] + near_z[dz]) for dy, dc, dx, dz in FARTHEST]
    barrier = pltpu.get_barrier_semaphore()
    for partner in partners[:-1]:
        pl.semaphore_signal(barrier, inc=1, device_id=partner, device_id_type=MESH)

    early[0].wait()
    place = lax.broadcasted_iota(jnp.int32, (cap, items), 1)
    for at in range(devices):
        wanted = jnp.broadcast_to(fetch_ref[:, at : at + 1], (cap, items)) == place
        pick_ref[at * cap : (at + 1) * cap, :] = jnp.where(wanted, 1.0, 0.0).astype(BF16)

    early[1].wait()
    early[2].wait()
    for at in range(chunks):
        early[3 + at].wait()
        cut = slice(at * part, (at + 1) * part)
        hidden_ref[:, cut] = first_layer(feat_ref[...], w_in_ref[:, cut], bias_ref[:, cut])
    early[3 + chunks].wait()
    unit_ref[...] = normalised(jnp.dot(hidden_ref[...], w_out_ref[...], preferred_element_type=F32))
    group = pool_count * cap
    for at in range(user_count):
        rows = slice(at * group, (at + 1) * group)
        outgoing_ref[rows, :] = jnp.dot(pick_ref[rows, :], unit_ref[...], preferred_element_type=F32).astype(BF16)
    pl.semaphore_wait(barrier, devices - 1)

    for turn, (to_user, to_pool) in enumerate(partners[:-1]):
        source = pl.multiple_of((to_user * pool_count + to_pool) * cap, cap)
        pltpu.make_async_remote_copy(
            src_ref=outgoing_ref.at[pl.ds(source, cap)],
            dst_ref=received_ref.at[pl.ds(turn * cap, cap)],
            send_sem=item_send,
            recv_sem=item_recv.at[turn // pool_count],
            device_id=(to_user, to_pool),
            device_id_type=MESH,
        ).start()
    own = pl.multiple_of((u * pool_count + p) * cap, cap)
    keep = pltpu.make_async_copy(
        outgoing_ref.at[pl.ds(own, cap)], received_ref.at[pl.ds((devices - 1) * cap, cap)], item_local
    )
    keep.start()

    def places(slot):
        code = ((y - slot // 512) & 3) * 32 + ((c - slot // 256) & 1) * 16
        code = code + ((x - slot // 64) & 3) * 4 + ((z - slot // 16) & 3)
        rows, events = slot.shape
        table = jnp.broadcast_to(turn_ref[...], (rows, LO))
        turns = [
            jnp.take_along_axis(table, code[:, at : at + LO], axis=1) for at in range(0, events, LO)
        ]
        return jnp.concatenate(turns, axis=1) * cap + slot % cap

    for load in late:
        load.wait()
    lane = lax.broadcasted_iota(jnp.int32, (1, LO), 1)
    ids = jnp.concatenate([label_id_ref[...].astype(F32)] * spread, axis=1)
    id_ref[p] = jnp.broadcast_to(jnp.where(lane // users == p % spread, ids, 0.0), (8, LO))
    info_ref[u] = jnp.concatenate(
        [neg_id_ref[...].astype(F32), jnp.log(neg_count_ref[...].astype(F32)), jnp.zeros((6, LO), F32)], axis=0
    )
    negatives = neg_feat_ref.shape[0]
    hidden_ref[:negatives] = first_layer(neg_feat_ref[...], w_in_ref[...], bias_ref[...])
    neg_ref[u] = normalised(jnp.dot(hidden_ref[:negatives], w_out_ref[...], preferred_element_type=F32))
    place_ref[...] = places(index_ref[...])
    label_wide = jnp.concatenate([label_ref[...]] * spread, axis=1)
    label_place = places(jnp.broadcast_to(label_wide, (8, LO)))[0:1, :users]
    prepare_route(place_ref, length_ref, init_ref, low_ref, high_ref, logit_ref)
    spread_weights(low_ref, high_ref, logit_ref, weight_ref, slot_ref, wide_ref)

    def along_user(ref, send_sem, recv_sem, step):
        return pltpu.make_async_remote_copy(
            src_ref=ref.at[u], dst_ref=ref.at[u], send_sem=send_sem, recv_sem=recv_sem,
            device_id=((u + step) % user_count, p), device_id_type=MESH,
        )

    def along_pool(ref, send_sem, recv_sem, step):
        return pltpu.make_async_remote_copy(
            src_ref=ref.at[p], dst_ref=ref.at[p], send_sem=send_sem, recv_sem=recv_sem,
            device_id=(u, (p + step) % pool_count), device_id_type=MESH,
        )

    def wait_recv(ref, sem):
        pltpu.make_async_remote_copy(
            src_ref=ref, dst_ref=ref, send_sem=sem, recv_sem=sem, device_id=(u, p), device_id_type=MESH
        ).wait_recv()

    def wait_send(ref, sem):
        pltpu.make_async_remote_copy(
            src_ref=ref, dst_ref=ref, send_sem=sem, recv_sem=sem, device_id=(u, p), device_id_type=MESH
        ).wait_send()

    def take(r):
        cut = pl.ds(pl.multiple_of(r * group, group), group)
        mapped_ref[cut, :] = jnp.dot(
            received_ref[cut, :], bilinear_ref[...], preferred_element_type=F32
        ).astype(BF16)
        return jnp.dot(wide_ref[:, cut], mapped_ref[cut, :], preferred_element_type=F32)

    both_ref[...] = jnp.zeros_like(both_ref)

    def take_round(r, carry):
        wait_recv(received_ref.at[pl.ds(pl.multiple_of(r * group, group), group)], item_recv.at[r])
        both_ref[...] += take(r)
        return carry

    lax.fori_loop(0, user_count - 1, take_round, 0)
    keep.wait()
    wait_recv(received_ref.at[pl.ds(0, group - cap)], item_recv.at[user_count - 1])
    both_ref[...] += take(user_count - 1)

    def send_negatives(step, carry):
        along_user(neg_ref, neg_send, neg_recv, step).start()
        along_user(info_ref, info_send, info_recv, step).start()
        return carry

    lax.fori_loop(1, user_count, send_negatives, 0)

    def send_ids(step, carry):
        along_pool(id_ref, id_send, id_recv, step).start()
        return carry

    lax.fori_loop(1, pool_count, send_ids, 0)

    capsules = squash(both_ref[...])
    for _ in range(1, ITERS):
        add_agreement(capsules, place_ref, mapped_ref, score_ref, logit_ref)
        spread_weights(low_ref, high_ref, logit_ref, weight_ref, slot_ref, wide_ref)
        capsules = squash(jnp.dot(wide_ref[...], mapped_ref[...], preferred_element_type=F32))
    user_vec, positive = attend(capsules, received_ref, label_place, count_ref)
    vec_ref[p] = user_vec

    def send_vec(step, carry):
        along_pool(vec_ref, vec_send, vec_recv.at[p // spread], step).start()
        return carry

    lax.fori_loop(1, pool_count, send_vec, 0)
    for k in range(INTERESTS):
        result_ref[:users, k * width : (k + 1) * width] = capsules[k * users : (k + 1) * users]
    wait_recv(info_ref.at[pl.ds(0, user_count - 1)], info_recv)
    wait_recv(id_ref.at[pl.ds(0, pool_count - 1)], id_recv)
    wait_recv(neg_ref.at[pl.ds(0, user_count - 1)], neg_recv)
    neg_ids = jnp.concatenate([column(info_ref[at, 0:1, :]) for at in range(user_count)], axis=0)
    neg_logs = jnp.concatenate([column(info_ref[at, 1:2, :]) for at in range(user_count)], axis=0)
    neg_rows = neg_ref[...].reshape(user_count * negatives, width)

    def one_line(line, own_line):
        first = pl.multiple_of(line * spread, spread)
        wait_recv(vec_ref.at[pl.ds(0, spread - 1 if own_line else spread)], vec_recv.at[line])
        vecs = vec_ref[pl.ds(first, spread)].reshape(LO, width)
        line_ids = id_ref[first, 0:1, :]
        for at in range(1, spread):
            line_ids = line_ids + id_ref[first + at, 0:1, :]
        logits = logit_scale * nt_dot(neg_rows, vecs) - neg_logs
        kept = jnp.where(neg_ids != line_ids, jnp.exp(logits), 0.0)
        partial_ref[line] = jnp.broadcast_to(jnp.sum(kept, axis=0, keepdims=True), (8, LO))

    def send_sum(line, to_pool):
        pltpu.make_async_remote_copy(
            src_ref=partial_ref.at[line], dst_ref=sum_ref.at[p], send_sem=sum_send, recv_sem=sum_recv,
            device_id=(u, to_pool), device_id_type=MESH,
        ).start()

    own_line = p // spread
    one_line(own_line, True)
    sum_ref[p] = partial_ref[own_line]

    def send_own(step, carry):
        send_sum(own_line, own_line * spread + (p + step) % spread)
        return carry

    lax.fori_loop(1, spread, send_own, 0)

    def other_line(step, carry):
        line = (own_line + step) % lines
        one_line(line, False)

        def send_other(at, carry):
            send_sum(line, line * spread + (p + at) % spread)
            return carry

        lax.fori_loop(0, spread, send_other, 0)
        return carry

    lax.fori_loop(1, lines, other_line, 0)
    wait_recv(sum_ref.at[pl.ds(0, pool_count - 1)], sum_recv)
    negative = sum_ref[0]
    for at in range(1, pool_count):
        negative = negative + sum_ref[at]
    mine = lax.broadcasted_iota(jnp.int32, (users, LO), 1) == (
        lax.broadcasted_iota(jnp.int32, (users, LO), 0) + (p % spread) * users
    )
    negative = jnp.sum(
        jnp.where(mine, jnp.broadcast_to(negative[0:1], (users, LO)), 0.0), axis=1, keepdims=True
    )
    loss = jnp.log(jnp.exp(positive) + negative) - positive
    eye = lax.broadcasted_iota(jnp.int32, (users, users), 0) == lax.broadcasted_iota(jnp.int32, (users, users), 1)
    loss = jnp.sum(jnp.where(eye, jnp.broadcast_to(loss, (users, users)), 0.0), axis=0, keepdims=True)
    result_ref[users:, :users] = jnp.broadcast_to(loss, (8, users))

    wait_send(outgoing_ref.at[pl.ds(0, (devices - 1) * cap)], item_send)
    wait_send(neg_ref.at[pl.ds(0, user_count - 1)], neg_send)
    wait_send(info_ref.at[pl.ds(0, user_count - 1)], info_send)
    wait_send(id_ref.at[pl.ds(0, pool_count - 1)], id_send)
    wait_send(vec_ref.at[pl.ds(0, pool_count - 1)], vec_send)
    wait_send(sum_ref.at[pl.ds(0, pool_count - 1)], sum_send)


def solution(mesh):
    both = ("user", "pool")
    user_count, pool_count = mesh.shape["user"], mesh.shape["pool"]

    def on_device(
        item_feats, w_in, bias_in, w_out, bilinear, fetch_table, hist_index, hist_len, route_init,
        label_index, label_ids, label_counts, neg_feats, neg_ids, neg_counts,
    ):
        users, events = hist_index.shape
        items, width = item_feats.shape
        hidden = w_in.shape[1]
        devices, _, cap = fetch_table.shape
        slots = devices * cap
        highs = slots // LO
        rows = INTERESTS * users
        negatives = neg_feats.shape[0]
        hbm = pl.BlockSpec(memory_space=pltpu.HBM)
        dma = pltpu.SemaphoreType.DMA
        operands = (
            item_feats, w_in, bias_in.reshape(1, -1), w_out, bilinear, fetch_table[:, 0, :].T, hist_index,
            hist_len.reshape(1, -1), route_init, label_index.reshape(1, -1), label_ids.reshape(1, -1),
            label_counts.reshape(1, -1), neg_feats, neg_ids.reshape(1, -1), neg_counts.reshape(1, -1),
            jnp.array([TURN], jnp.int32),
        )
        result = pl.pallas_call(
            functools.partial(step_kernel, user_count, pool_count),
            out_shape=jax.ShapeDtypeStruct((users + 8, INTERESTS * width), F32),
            in_specs=[hbm] * len(operands),
            out_specs=pl.BlockSpec(memory_space=pltpu.VMEM),
            scratch_shapes=[pltpu.VMEM(operand.shape, operand.dtype) for operand in operands] + [
                pltpu.VMEM((slots, items), BF16),
                pltpu.VMEM((items, hidden), BF16),
                pltpu.VMEM((items, width), BF16),
                pltpu.VMEM((slots, width), BF16),
                pltpu.VMEM((slots, width), BF16),
                pltpu.VMEM((slots, width), BF16),
                pltpu.VMEM((users, events), jnp.int32),
                pltpu.VMEM((users, LO, events), BF16),
                pltpu.VMEM((users, highs, events), F32),
                pltpu.VMEM((INTERESTS + 1, users, events), F32),
                pltpu.VMEM((INTERESTS, users, events), F32),
                pltpu.VMEM((rows * highs, LO), F32),
                pltpu.VMEM((2 * rows, slots), BF16),
                pltpu.VMEM((2 * rows, width), F32),
                pltpu.VMEM((rows, slots), F32),
                pltpu.VMEM((user_count, negatives, width), BF16),
                pltpu.VMEM((user_count, 8, LO), F32),
                pltpu.VMEM((pool_count, 8, LO), F32),
                pltpu.VMEM((pool_count, users, width), BF16),
                pltpu.VMEM((pool_count * users // LO, 8, LO), F32),
                pltpu.VMEM((pool_count, 8, LO), F32),
                dma((19,)),
                dma, dma((user_count,)), dma, dma, dma, dma, dma, dma, dma,
                dma, dma((pool_count * users // LO,)), dma, dma,
            ],
            compiler_params=pltpu.CompilerParams(
                collective_id=0, has_side_effects=True, vmem_limit_bytes=60 << 20
            ),
        )(*operands)
        return result[:users], result[users, :users]

    in_specs = (
        P(both, None), P(), P(), P(), P(), P(None, both, None), P(both, None), P(both),
        P(both, None, None), P(both), P(both), P(both), P(both, None), P(both), P(both),
    )
    out_specs = (P(both, None), P(both))
    return jax.shard_map(on_device, mesh=mesh, in_specs=in_specs, out_specs=out_specs, check_vma=False)
```

```python
import functools

import jax
import jax.numpy as jnp
from jax import lax
from jax.experimental import pallas as pl
from jax.experimental.pallas import tpu as pltpu
from jax.sharding import PartitionSpec as P

INTERESTS = 4
ITERS = 3
LO = 128

norm_epsilon = 1e-06
attend_scale = 8.0
logit_scale = 20.0

F32 = jnp.float32
BF16 = jnp.bfloat16


MESH = pl.DeviceIdType.MESH


HOPS = (0, 1, 2, 1)
FARTHEST = sorted(
    ((dy, dc, dx, dz) for dy in range(4) for dc in range(2) for dx in range(4) for dz in range(4)),
    key=lambda d: (-HOPS[d[0]] - HOPS[d[2]] - HOPS[d[3]], (d[0] + d[2] + d[3]) % 4, -d[1]),
)
TURN = [0] * len(FARTHEST)
for turn, (dy, dc, dx, dz) in enumerate(FARTHEST):
    TURN[((dy * 2 + dc) * 4 + dx) * 4 + dz] = turn


def normalised(embedding):
    inverse_norm = lax.rsqrt(jnp.sum(embedding * embedding, axis=1, keepdims=True) + norm_epsilon)
    return (embedding * inverse_norm).astype(BF16)


def first_layer(features, w_in, bias):
    hidden = jnp.dot(features, w_in, preferred_element_type=F32) + bias
    return jnp.maximum(hidden, 0.0).astype(BF16)


def nt_dot(a, b):
    return lax.dot_general(a, b, (((1,), (1,)), ((), ())), preferred_element_type=F32)


def column(row):
    size = row.shape[1]
    wide = jnp.broadcast_to(row.astype(F32), (size, size))
    eye = lax.broadcasted_iota(jnp.int32, (size, size), 0) == lax.broadcasted_iota(jnp.int32, (size, size), 1)
    return jnp.sum(jnp.where(eye, wide, 0.0), axis=1, keepdims=True)


def prepare_route(place_ref, length_ref, init_ref, low_ref, high_ref, logit_ref):
    users, events = place_ref.shape
    highs = high_ref.shape[1]
    live = lax.broadcasted_iota(jnp.int32, (users, events), 1).astype(F32) < column(length_ref[...])
    logit_ref[INTERESTS] = jnp.where(live, place_ref[...], -1).astype(F32)
    for k in range(INTERESTS):
        logit_ref[k] = init_ref[:, k, :]

    def one_user(n, carry):
        low = jnp.broadcast_to(place_ref[pl.ds(n, 1), :] & (LO - 1), (LO, events))
        marks = jnp.where(low == lax.broadcasted_iota(jnp.int32, (LO, events), 0), 1.0, 0.0)
        low_ref[n] = marks.T.astype(BF16)
        high = jnp.broadcast_to(logit_ref[INTERESTS, pl.ds(n, 1), :], (highs, events))
        first = (lax.broadcasted_iota(jnp.int32, (highs, events), 0) * LO).astype(F32)
        high_ref[n] = jnp.where((high >= first) & (high < first + LO), 1.0, 0.0)
        return carry

    lax.fori_loop(0, users, one_user, 0, unroll=4)


def spread_weights(low_ref, high_ref, logit_ref, weight_ref, slot_ref, wide_ref):
    _, users, events = weight_ref.shape
    highs = high_ref.shape[1]
    rows = INTERESTS * users
    raised = [jnp.exp(logit_ref[k]) for k in range(INTERESTS)]
    total = raised[0] + raised[1] + raised[2] + raised[3]
    for k in range(INTERESTS):
        weight_ref[k] = (raised[k] / total).astype(BF16).astype(F32)

    def one_user(n, carry):
        mask = high_ref[n]
        spread = [
            (jnp.broadcast_to(weight_ref[k, pl.ds(n, 1), :], (highs, events)) * mask).astype(BF16)
            for k in range(INTERESTS)
        ]
        summed = jnp.dot(jnp.concatenate(spread, axis=0), low_ref[n], preferred_element_type=F32)
        for k in range(INTERESTS):
            slot_ref[pl.ds(pl.multiple_of((k * users + n) * highs, highs), highs), :] = summed[
                k * highs : (k + 1) * highs
            ]
        return carry

    lax.fori_loop(0, users, one_user, 0, unroll=4)
    for high in range(highs):
        part = slot_ref[pl.ds(high, rows, stride=highs), :]
        upper = part.astype(BF16)
        wide_ref[:rows, high * LO : (high + 1) * LO] = upper
        wide_ref[rows:, high * LO : (high + 1) * LO] = (part - upper.astype(F32)).astype(BF16)


def squash(both):
    rows = both.shape[0] // 2
    sums = both[:rows] + both[rows:]
    norm_sq = jnp.sum(sums * sums, axis=1, keepdims=True)
    return sums * jnp.sqrt(norm_sq) / (1.0 + norm_sq)


def add_agreement(capsules, place_ref, turned_ref, score_ref, logit_ref):
    users, events = place_ref.shape
    highs = turned_ref.shape[1] // LO
    score_ref[...] = jnp.dot(capsules.astype(BF16), turned_ref[...], preferred_element_type=F32)
    for group in range(users // 8):
        for chunk in range(events // LO):
            at = place_ref[group * 8 : group * 8 + 8, chunk * LO : (chunk + 1) * LO]
            low = at & (LO - 1)
            block = at >> 7
            found = [jnp.zeros((8, LO), F32)] * INTERESTS
            for high in range(highs):
                here = block == high
                for k in range(INTERESTS):
                    scores = score_ref[
                        k * users + group * 8 : k * users + group * 8 + 8, high * LO : (high + 1) * LO
                    ]
                    picked = jnp.take_along_axis(scores, low, axis=1)
                    found[k] = jnp.where(here, picked, found[k])
            for k in range(INTERESTS):
                logit_ref[k, group * 8 : group * 8 + 8, chunk * LO : (chunk + 1) * LO] += found[k]


def attend(capsules, received_ref, label_place, count_ref):
    users = label_place.shape[1]
    slots = received_ref.shape[0]
    wanted = lax.broadcasted_iota(jnp.int32, (users, slots), 1).astype(F32) == column(label_place)
    label_rows = jnp.dot(
        jnp.where(wanted, 1.0, 0.0).astype(BF16), received_ref[...], preferred_element_type=F32
    )
    each = [capsules[k * users : (k + 1) * users] for k in range(INTERESTS)]
    raised = [jnp.exp(attend_scale * jnp.sum(c * label_rows, axis=1, keepdims=True)) for c in each]
    total = raised[0] + raised[1] + raised[2] + raised[3]
    user_vec = (raised[0] / total) * each[0]
    for k in range(1, INTERESTS):
        user_vec = user_vec + (raised[k] / total) * each[k]
    user_vec = user_vec.astype(BF16)
    positive = logit_scale * jnp.sum(user_vec.astype(F32) * label_rows, axis=1, keepdims=True) - jnp.log(
        column(count_ref[...])
    )
    return user_vec, positive


def step_kernel(
    user_count, pool_count,
    feat_hbm, w_in_hbm, bias_hbm, w_out_hbm, bilinear_hbm, fetch_hbm, index_hbm, length_hbm, init_hbm,
    label_hbm, label_id_hbm, count_hbm, neg_feat_hbm, neg_id_hbm, neg_count_hbm, turn_hbm,
    interest_hbm, loss_ref,
    feat_ref, w_in_ref, bias_ref, w_out_ref, bilinear_ref, fetch_ref, index_ref, length_ref, init_ref,
    label_ref, label_id_ref, count_ref, neg_feat_ref, neg_id_ref, neg_count_ref, turn_ref, pick_ref, hidden_ref, unit_ref, outgoing_ref, received_ref,
    mapped_ref, turned_ref, place_ref, low_ref, high_ref, logit_ref, weight_ref, slot_ref, wide_ref, both_ref, score_ref,
    interest_ref, neg_ref, info_ref, id_ref, vec_ref, partial_ref, sum_ref,
    load_sem, item_send, item_recv, item_local, neg_send, neg_recv, side_send, side_recv, store_sem, info_send, info_recv,
    id_send, id_recv, vec_send, vec_recv, sum_send, sum_recv,
):
    u = lax.axis_index("user")
    p = lax.axis_index("pool")
    devices = user_count * pool_count
    cap = fetch_ref.shape[0]
    users, width = vec_ref.shape[1], vec_ref.shape[2]
    items = unit_ref.shape[0]
    hidden = w_in_ref.shape[1]
    chunks = 4
    part = hidden // chunks
    spread = LO // users

    early = [pltpu.make_async_copy(fetch_hbm, fetch_ref, load_sem.at[0])]
    early.append(pltpu.make_async_copy(feat_hbm, feat_ref, load_sem.at[1]))
    early.append(pltpu.make_async_copy(bias_hbm, bias_ref, load_sem.at[2]))
    for at in range(chunks):
        cut = pl.ds(at * part, part)
        early.append(pltpu.make_async_copy(w_in_hbm.at[:, cut], w_in_ref.at[:, cut], load_sem.at[3 + at]))
    early.append(pltpu.make_async_copy(w_out_hbm, w_out_ref, load_sem.at[3 + chunks]))
    pairs = [
        (neg_feat_hbm, neg_feat_ref), (index_hbm, index_ref), (length_hbm, length_ref), (init_hbm, init_ref),
        (label_hbm, label_ref), (label_id_hbm, label_id_ref), (count_hbm, count_ref), (neg_id_hbm, neg_id_ref),
        (neg_count_hbm, neg_count_ref), (turn_hbm, turn_ref), (bilinear_hbm, bilinear_ref),
    ]
    late = [
        pltpu.make_async_copy(source, target, load_sem.at[4 + chunks + at])
        for at, (source, target) in enumerate(pairs)
    ]
    for load in early + late:
        load.start()

    y, c, x, z = u // 2, u % 2, p // 4, p % 4
    near_y = [((y + d) % 4) * 2 for d in range(4)]
    near_c = [c, 1 - c]
    near_x = [((x + d) % 4) * 4 for d in range(4)]
    near_z = [(z + d) % 4 for d in range(4)]
    partners = [(near_y[dy] + near_c[dc], near_x[dx] + near_z[dz]) for dy, dc, dx, dz in FARTHEST]
    barrier = pltpu.get_barrier_semaphore()
    for partner in partners[:-1]:
        pl.semaphore_signal(barrier, inc=1, device_id=partner, device_id_type=MESH)

    early[0].wait()
    place = lax.broadcasted_iota(jnp.int32, (cap, items), 1)
    for at in range(devices):
        wanted = jnp.broadcast_to(fetch_ref[:, at : at + 1], (cap, items)) == place
        pick_ref[at * cap : (at + 1) * cap, :] = jnp.where(wanted, 1.0, 0.0).astype(BF16)

    early[1].wait()
    early[2].wait()
    for at in range(chunks):
        early[3 + at].wait()
        cut = slice(at * part, (at + 1) * part)
        hidden_ref[:, cut] = first_layer(feat_ref[...], w_in_ref[:, cut], bias_ref[:, cut])
    early[3 + chunks].wait()
    unit_ref[...] = normalised(jnp.dot(hidden_ref[...], w_out_ref[...], preferred_element_type=F32))
    group = pool_count * cap
    for at in range(user_count):
        rows = slice(at * group, (at + 1) * group)
        outgoing_ref[rows, :] = jnp.dot(pick_ref[rows, :], unit_ref[...], preferred_element_type=F32).astype(BF16)
    pl.semaphore_wait(barrier, devices - 1)

    for turn, (to_user, to_pool) in enumerate(partners[:-1]):
        source = pl.multiple_of((to_user * pool_count + to_pool) * cap, cap)
        pltpu.make_async_remote_copy(
            src_ref=outgoing_ref.at[pl.ds(source, cap)],
            dst_ref=received_ref.at[pl.ds(turn * cap, cap)],
            send_sem=item_send,
            recv_sem=item_recv.at[turn // pool_count],
            device_id=(to_user, to_pool),
            device_id_type=MESH,
        ).start()
    own = pl.multiple_of((u * pool_count + p) * cap, cap)
    keep = pltpu.make_async_copy(
        outgoing_ref.at[pl.ds(own, cap)], received_ref.at[pl.ds((devices - 1) * cap, cap)], item_local
    )
    keep.start()

    def places(slot):
        code = ((y - slot // 512) & 3) * 32 + ((c - slot // 256) & 1) * 16
        code = code + ((x - slot // 64) & 3) * 4 + ((z - slot // 16) & 3)
        rows, events = slot.shape
        table = jnp.broadcast_to(turn_ref[...], (rows, LO))
        turns = [
            jnp.take_along_axis(table, code[:, at : at + LO], axis=1) for at in range(0, events, LO)
        ]
        return jnp.concatenate(turns, axis=1) * cap + slot % cap

    for load in late:
        load.wait()
    lane = lax.broadcasted_iota(jnp.int32, (1, LO), 1)
    ids = jnp.concatenate([label_id_ref[...].astype(F32)] * spread, axis=1)
    id_ref[p] = jnp.broadcast_to(jnp.where(lane // users == p % spread, ids, 0.0), (8, LO))
    info_ref[u] = jnp.concatenate(
        [neg_id_ref[...].astype(F32), jnp.log(neg_count_ref[...].astype(F32)), jnp.zeros((6, LO), F32)], axis=0
    )
    negatives = neg_feat_ref.shape[0]
    hidden_ref[:negatives] = first_layer(neg_feat_ref[...], w_in_ref[...], bias_ref[...])
    neg_ref[u] = normalised(jnp.dot(hidden_ref[:negatives], w_out_ref[...], preferred_element_type=F32))
    place_ref[...] = places(index_ref[...])
    label_wide = jnp.concatenate([label_ref[...]] * spread, axis=1)
    label_place = places(jnp.broadcast_to(label_wide, (8, LO)))[0:1, :users]
    prepare_route(place_ref, length_ref, init_ref, low_ref, high_ref, logit_ref)
    spread_weights(low_ref, high_ref, logit_ref, weight_ref, slot_ref, wide_ref)

    def along_user(ref, send_sem, recv_sem, step):
        return pltpu.make_async_remote_copy(
            src_ref=ref.at[u], dst_ref=ref.at[u], send_sem=send_sem, recv_sem=recv_sem,
            device_id=((u + step) % user_count, p), device_id_type=MESH,
        )

    def along_pool(ref, send_sem, recv_sem, step):
        return pltpu.make_async_remote_copy(
            src_ref=ref.at[p], dst_ref=ref.at[p], send_sem=send_sem, recv_sem=recv_sem,
            device_id=(u, (p + step) % pool_count), device_id_type=MESH,
        )

    def wait_recv(ref, sem):
        pltpu.make_async_remote_copy(
            src_ref=ref, dst_ref=ref, send_sem=sem, recv_sem=sem, device_id=(u, p), device_id_type=MESH
        ).wait_recv()

    def wait_send(ref, sem):
        pltpu.make_async_remote_copy(
            src_ref=ref, dst_ref=ref, send_sem=sem, recv_sem=sem, device_id=(u, p), device_id_type=MESH
        ).wait_send()

    def take(r):
        cut = pl.ds(pl.multiple_of(r * group, group), group)
        mapped = jnp.dot(received_ref[cut, :], bilinear_ref[...], preferred_element_type=F32)
        mapped_ref[cut, :] = mapped.astype(BF16)
        turned_ref[:, cut] = mapped.T.astype(BF16)
        return jnp.dot(wide_ref[:, cut], mapped_ref[cut, :], preferred_element_type=F32)

    both_ref[...] = jnp.zeros_like(both_ref)

    def take_round(r, carry):
        wait_recv(received_ref.at[pl.ds(pl.multiple_of(r * group, group), group)], item_recv.at[r])
        both_ref[...] += take(r)
        return carry

    lax.fori_loop(0, user_count - 1, take_round, 0)
    keep.wait()
    wait_recv(received_ref.at[pl.ds(0, group - cap)], item_recv.at[user_count - 1])
    both_ref[...] += take(user_count - 1)

    def negative_block(block, to_user, send_sem, recv_sem):
        return pltpu.make_async_remote_copy(
            src_ref=neg_ref.at[block], dst_ref=neg_ref.at[block], send_sem=send_sem, recv_sem=recv_sem,
            device_id=(to_user, p), device_id_type=MESH,
        )

    sibling = y * 2 + near_c[1]
    around = [near_y[step] + c for step in (2, 1, 3)]
    for to_user in around:
        negative_block(u, to_user, neg_send, neg_recv).start()
    negative_block(u, sibling, side_send, side_recv).start()

    def send_info(step, carry):
        along_user(info_ref, info_send, info_recv, step).start()
        return carry

    lax.fori_loop(1, user_count, send_info, 0)

    def send_ids(step, carry):
        along_pool(id_ref, id_send, id_recv, step).start()
        return carry

    lax.fori_loop(1, pool_count, send_ids, 0)

    capsules = squash(both_ref[...])
    for _ in range(1, ITERS):
        add_agreement(capsules, place_ref, turned_ref, score_ref, logit_ref)
        spread_weights(low_ref, high_ref, logit_ref, weight_ref, slot_ref, wide_ref)
        capsules = squash(jnp.dot(wide_ref[...], mapped_ref[...], preferred_element_type=F32))
    wait_recv(neg_ref.at[pl.ds(0, len(around))], neg_recv)
    for from_user in around:
        negative_block(from_user, sibling, side_send, side_recv).start()
    user_vec, positive = attend(capsules, received_ref, label_place, count_ref)
    vec_ref[p] = user_vec

    row = [(dx, dz) for dx in (2, 1, 3, 0) for dz in (2, 1, 3, 0) if dx or dz]
    for dx, dz in row:
        pltpu.make_async_remote_copy(
            src_ref=vec_ref.at[p], dst_ref=vec_ref.at[p], send_sem=vec_send, recv_sem=vec_recv.at[x],
            device_id=(u, near_x[dx] + near_z[dz]), device_id_type=MESH,
        ).start()
    for k in range(INTERESTS):
        interest_ref[:, k * width : (k + 1) * width] = capsules[k * users : (k + 1) * users]
    store = pltpu.make_async_copy(interest_ref, interest_hbm, store_sem)
    store.start()
    wait_recv(info_ref.at[pl.ds(0, user_count - 1)], info_recv)
    wait_recv(id_ref.at[pl.ds(0, pool_count - 1)], id_recv)
    wait_recv(neg_ref.at[pl.ds(0, 1 + len(around))], side_recv)
    neg_ids = jnp.concatenate([column(info_ref[at, 0:1, :]) for at in range(user_count)], axis=0)
    neg_logs = jnp.concatenate([column(info_ref[at, 1:2, :]) for at in range(user_count)], axis=0)
    neg_rows = neg_ref[...].reshape(user_count * negatives, width)

    def one_line(line, own_line):
        first = pl.multiple_of(line * spread, spread)
        wait_recv(vec_ref.at[pl.ds(0, spread - 1 if own_line else spread)], vec_recv.at[line])
        vecs = vec_ref[pl.ds(first, spread)].reshape(LO, width)
        line_ids = id_ref[first, 0:1, :]
        for at in range(1, spread):
            line_ids = line_ids + id_ref[first + at, 0:1, :]
        logits = logit_scale * nt_dot(neg_rows, vecs) - neg_logs
        kept = jnp.where(neg_ids != line_ids, jnp.exp(logits), 0.0)
        partial_ref[line] = jnp.broadcast_to(jnp.sum(kept, axis=0, keepdims=True), (8, LO))

    for dx in (2, 1, 3, 0):
        line = near_x[dx] // spread
        one_line(line, dx == 0)
        for dz in (2, 1, 3, 0):
            if dx or dz:
                pltpu.make_async_remote_copy(
                    src_ref=partial_ref.at[line], dst_ref=sum_ref.at[p], send_sem=sum_send, recv_sem=sum_recv,
                    device_id=(u, near_x[dx] + near_z[dz]), device_id_type=MESH,
                ).start()
    sum_ref[p] = partial_ref[x]
    wait_recv(sum_ref.at[pl.ds(0, pool_count - 1)], sum_recv)
    negative = sum_ref[0]
    for at in range(1, pool_count):
        negative = negative + sum_ref[at]
    mine = lax.broadcasted_iota(jnp.int32, (users, LO), 1) == (
        lax.broadcasted_iota(jnp.int32, (users, LO), 0) + (p % spread) * users
    )
    negative = jnp.sum(
        jnp.where(mine, jnp.broadcast_to(negative[0:1], (users, LO)), 0.0), axis=1, keepdims=True
    )
    loss = jnp.log(jnp.exp(positive) + negative) - positive
    eye = lax.broadcasted_iota(jnp.int32, (users, users), 0) == lax.broadcasted_iota(jnp.int32, (users, users), 1)
    loss_ref[...] = jnp.sum(jnp.where(eye, jnp.broadcast_to(loss, (users, users)), 0.0), axis=0, keepdims=True)

    wait_send(outgoing_ref.at[pl.ds(0, (devices - 1) * cap)], item_send)
    wait_send(neg_ref.at[pl.ds(0, len(around))], neg_send)
    wait_send(neg_ref.at[pl.ds(0, 1 + len(around))], side_send)
    store.wait()
    wait_send(info_ref.at[pl.ds(0, user_count - 1)], info_send)
    wait_send(id_ref.at[pl.ds(0, pool_count - 1)], id_send)
    wait_send(vec_ref.at[pl.ds(0, pool_count - 1)], vec_send)
    wait_send(sum_ref.at[pl.ds(0, pool_count - 1)], sum_send)


def hand_out(interest_ref, loss_ref, interest_out, loss_out):
    interest_out[...] = interest_ref[...]
    loss_out[...] = loss_ref[...]


def solution(mesh):
    both = ("user", "pool")
    user_count, pool_count = mesh.shape["user"], mesh.shape["pool"]

    def on_device(
        item_feats, w_in, bias_in, w_out, bilinear, fetch_table, hist_index, hist_len, route_init,
        label_index, label_ids, label_counts, neg_feats, neg_ids, neg_counts,
    ):
        users, events = hist_index.shape
        items, width = item_feats.shape
        hidden = w_in.shape[1]
        devices, _, cap = fetch_table.shape
        slots = devices * cap
        highs = slots // LO
        rows = INTERESTS * users
        negatives = neg_feats.shape[0]
        vmem = pl.BlockSpec(memory_space=pltpu.VMEM)
        hbm = pl.BlockSpec(memory_space=pltpu.HBM)
        dma = pltpu.SemaphoreType.DMA
        operands = (
            item_feats, w_in, bias_in.reshape(1, -1), w_out, bilinear, fetch_table[:, 0, :].T, hist_index,
            hist_len.reshape(1, -1), route_init, label_index.reshape(1, -1), label_ids.reshape(1, -1),
            label_counts.reshape(1, -1), neg_feats, neg_ids.reshape(1, -1), neg_counts.reshape(1, -1),
            jnp.array([TURN], jnp.int32),
        )
        shapes = (
            jax.ShapeDtypeStruct((users, INTERESTS * width), F32),
            jax.ShapeDtypeStruct((1, users), F32),
        )
        results = pl.pallas_call(
            functools.partial(step_kernel, user_count, pool_count),
            out_shape=shapes,
            in_specs=[hbm] * len(operands),
            out_specs=(hbm, pl.BlockSpec(memory_space=pltpu.VMEM)),
            scratch_shapes=[pltpu.VMEM(operand.shape, operand.dtype) for operand in operands] + [
                pltpu.VMEM((slots, items), BF16),
                pltpu.VMEM((items, hidden), BF16),
                pltpu.VMEM((items, width), BF16),
                pltpu.VMEM((slots, width), BF16),
                pltpu.VMEM((slots, width), BF16),
                pltpu.VMEM((slots, width), BF16),
                pltpu.VMEM((width, slots), BF16),
                pltpu.VMEM((users, events), jnp.int32),
                pltpu.VMEM((users, events, LO), BF16),
                pltpu.VMEM((users, highs, events), F32),
                pltpu.VMEM((INTERESTS + 1, users, events), F32),
                pltpu.VMEM((INTERESTS, users, events), F32),
                pltpu.VMEM((rows * highs, LO), F32),
                pltpu.VMEM((2 * rows, slots), BF16),
                pltpu.VMEM((2 * rows, width), F32),
                pltpu.VMEM((rows, slots), F32),
                pltpu.VMEM((users, INTERESTS * width), F32),
                pltpu.VMEM((user_count, negatives, width), BF16),
                pltpu.VMEM((user_count, 8, LO), F32),
                pltpu.VMEM((pool_count, 8, LO), F32),
                pltpu.VMEM((pool_count, users, width), BF16),
                pltpu.VMEM((pool_count * users // LO, 8, LO), F32),
                pltpu.VMEM((pool_count, 8, LO), F32),
                dma((19,)),
                dma, dma((user_count,)), dma, dma, dma, dma, dma, dma, dma, dma, dma, dma,
                dma, dma((pool_count * users // LO,)), dma, dma,
            ],
            compiler_params=pltpu.CompilerParams(
                collective_id=0, has_side_effects=True, vmem_limit_bytes=60 << 20
            ),
        )(*operands)
        interests, loss = pl.pallas_call(
            hand_out, out_shape=shapes, in_specs=[vmem, vmem], out_specs=(vmem, vmem)
        )(*results)
        return interests, loss.reshape(users)

    in_specs = (
        P(both, None), P(), P(), P(), P(), P(None, both, None), P(both, None), P(both),
        P(both, None, None), P(both), P(both), P(both), P(both, None), P(both), P(both),
    )
    out_specs = (P(both, None), P(both))
    return jax.shard_map(on_device, mesh=mesh, in_specs=in_specs, out_specs=out_specs, check_vma=False)
```

```python
import functools

import jax
import jax.numpy as jnp
from jax import lax
from jax.experimental import pallas as pl
from jax.experimental.pallas import tpu as pltpu
from jax.sharding import PartitionSpec as P

INTERESTS = 4
ITERS = 3
LO = 128

norm_epsilon = 1e-06
attend_scale = 8.0
logit_scale = 20.0

F32 = jnp.float32
BF16 = jnp.bfloat16


MESH = pl.DeviceIdType.MESH


HOPS = (0, 1, 2, 1)
FARTHEST = sorted(
    ((dy, dc, dx, dz) for dy in range(4) for dc in range(2) for dx in range(4) for dz in range(4)),
    key=lambda d: (-HOPS[d[0]] - HOPS[d[2]] - HOPS[d[3]], (d[0] + d[2] + d[3]) % 4, -d[1]),
)
TURN = [0] * len(FARTHEST)
for turn, (dy, dc, dx, dz) in enumerate(FARTHEST):
    TURN[((dy * 2 + dc) * 4 + dx) * 4 + dz] = turn


def normalised(embedding):
    inverse_norm = lax.rsqrt(jnp.sum(embedding * embedding, axis=1, keepdims=True) + norm_epsilon)
    return (embedding * inverse_norm).astype(BF16)


def first_layer(features, w_in, bias):
    hidden = jnp.dot(features, w_in, preferred_element_type=F32) + bias
    return jnp.maximum(hidden, 0.0).astype(BF16)


def nt_dot(a, b):
    return lax.dot_general(a, b, (((1,), (1,)), ((), ())), preferred_element_type=F32)


def column(row):
    size = row.shape[1]
    wide = jnp.broadcast_to(row.astype(F32), (size, size))
    eye = lax.broadcasted_iota(jnp.int32, (size, size), 0) == lax.broadcasted_iota(jnp.int32, (size, size), 1)
    return jnp.sum(jnp.where(eye, wide, 0.0), axis=1, keepdims=True)


def prepare_route(place_ref, length_ref, init_ref, low_ref, high_ref, logit_ref):
    users, events = place_ref.shape
    highs = high_ref.shape[1]
    live = lax.broadcasted_iota(jnp.int32, (users, events), 1).astype(F32) < column(length_ref[...])
    logit_ref[INTERESTS] = jnp.where(live, place_ref[...], -1).astype(F32)
    for k in range(INTERESTS):
        logit_ref[k] = init_ref[:, k, :]

    def one_user(n, carry):
        low = jnp.broadcast_to(place_ref[pl.ds(n, 1), :] & (LO - 1), (LO, events))
        marks = jnp.where(low == lax.broadcasted_iota(jnp.int32, (LO, events), 0), 1.0, 0.0)
        low_ref[n] = marks.T.astype(BF16)
        high = jnp.broadcast_to(logit_ref[INTERESTS, pl.ds(n, 1), :], (highs, events))
        first = (lax.broadcasted_iota(jnp.int32, (highs, events), 0) * LO).astype(F32)
        high_ref[n] = jnp.where((high >= first) & (high < first + LO), 1.0, 0.0)
        return carry

    lax.fori_loop(0, users, one_user, 0, unroll=4)


def spread_weights(low_ref, high_ref, logit_ref, weight_ref, slot_ref, wide_ref):
    _, users, events = weight_ref.shape
    highs = high_ref.shape[1]
    rows = INTERESTS * users
    raised = [jnp.exp(logit_ref[k]) for k in range(INTERESTS)]
    total = raised[0] + raised[1] + raised[2] + raised[3]
    for k in range(INTERESTS):
        weight_ref[k] = (raised[k] / total).astype(BF16).astype(F32)

    def one_user(n, carry):
        mask = high_ref[n]
        spread = [
            (jnp.broadcast_to(weight_ref[k, pl.ds(n, 1), :], (highs, events)) * mask).astype(BF16)
            for k in range(INTERESTS)
        ]
        summed = jnp.dot(jnp.concatenate(spread, axis=0), low_ref[n], preferred_element_type=F32)
        for k in range(INTERESTS):
            slot_ref[pl.ds(pl.multiple_of((k * users + n) * highs, highs), highs), :] = summed[
                k * highs : (k + 1) * highs
            ]
        return carry

    lax.fori_loop(0, users, one_user, 0, unroll=16)
    for high in range(highs):
        part = slot_ref[pl.ds(high, rows, stride=highs), :]
        upper = part.astype(BF16)
        wide_ref[:rows, high * LO : (high + 1) * LO] = upper
        wide_ref[rows:, high * LO : (high + 1) * LO] = (part - upper.astype(F32)).astype(BF16)


def squash(both):
    rows = both.shape[0] // 2
    sums = both[:rows] + both[rows:]
    norm_sq = jnp.sum(sums * sums, axis=1, keepdims=True)
    return sums * jnp.sqrt(norm_sq) / (1.0 + norm_sq)


def add_agreement(capsules, place_ref, turned_ref, score_ref, logit_ref):
    users, events = place_ref.shape
    highs = turned_ref.shape[1] // LO
    score_ref[...] = jnp.dot(capsules.astype(BF16), turned_ref[...], preferred_element_type=F32)
    for group in range(users // 8):
        for chunk in range(events // LO):
            at = place_ref[group * 8 : group * 8 + 8, chunk * LO : (chunk + 1) * LO]
            low = at & (LO - 1)
            block = at >> 7
            found = [jnp.zeros((8, LO), F32)] * INTERESTS
            for high in range(highs):
                here = block == high
                for k in range(INTERESTS):
                    scores = score_ref[
                        k * users + group * 8 : k * users + group * 8 + 8, high * LO : (high + 1) * LO
                    ]
                    picked = jnp.take_along_axis(scores, low, axis=1)
                    found[k] = jnp.where(here, picked, found[k])
            for k in range(INTERESTS):
                logit_ref[k, group * 8 : group * 8 + 8, chunk * LO : (chunk + 1) * LO] += found[k]


def attend(capsules, label_rows, count_log):
    users = label_rows.shape[0]
    each = [capsules[k * users : (k + 1) * users] for k in range(INTERESTS)]
    raised = [jnp.exp(attend_scale * jnp.sum(c * label_rows, axis=1, keepdims=True)) for c in each]
    total = raised[0] + raised[1] + raised[2] + raised[3]
    user_vec = (raised[0] / total) * each[0]
    for k in range(1, INTERESTS):
        user_vec = user_vec + (raised[k] / total) * each[k]
    user_vec = user_vec.astype(BF16)
    positive = logit_scale * jnp.sum(user_vec.astype(F32) * label_rows, axis=1, keepdims=True) - count_log
    return user_vec, positive


def step_kernel(
    user_count, pool_count,
    feat_hbm, w_in_hbm, bias_hbm, w_out_hbm, bilinear_hbm, fetch_hbm, index_hbm, length_hbm, init_hbm,
    label_hbm, label_id_hbm, count_hbm, neg_feat_hbm, neg_id_hbm, neg_count_hbm, turn_hbm,
    interest_hbm, loss_ref,
    feat_ref, w_in_ref, bias_ref, w_out_ref, bilinear_ref, fetch_ref, index_ref, length_ref, init_ref,
    label_ref, label_id_ref, count_ref, neg_feat_ref, neg_id_ref, neg_count_ref, turn_ref, pick_ref, hidden_ref, unit_ref, outgoing_ref, received_ref,
    mapped_ref, turned_ref, label_row_ref, place_ref, low_ref, high_ref, logit_ref, weight_ref, slot_ref, wide_ref, both_ref, score_ref,
    interest_ref, neg_ref, info_ref, id_ref, vec_ref, partial_ref, sum_ref,
    load_sem, item_send, item_recv, item_local, neg_send, neg_recv, side_send, side_recv, store_sem, info_send, info_recv,
    id_send, id_recv, vec_send, vec_recv, sum_send, sum_recv,
):
    u = lax.axis_index("user")
    p = lax.axis_index("pool")
    devices = user_count * pool_count
    cap = fetch_ref.shape[0]
    users, width = vec_ref.shape[1], vec_ref.shape[2]
    items = unit_ref.shape[0]
    hidden = w_in_ref.shape[1]
    chunks = 4
    part = hidden // chunks
    spread = LO // users

    early = [pltpu.make_async_copy(fetch_hbm, fetch_ref, load_sem.at[0])]
    early.append(pltpu.make_async_copy(feat_hbm, feat_ref, load_sem.at[1]))
    early.append(pltpu.make_async_copy(bias_hbm, bias_ref, load_sem.at[2]))
    for at in range(chunks):
        cut = pl.ds(at * part, part)
        early.append(pltpu.make_async_copy(w_in_hbm.at[:, cut], w_in_ref.at[:, cut], load_sem.at[3 + at]))
    early.append(pltpu.make_async_copy(w_out_hbm, w_out_ref, load_sem.at[3 + chunks]))
    pairs = [
        (neg_feat_hbm, neg_feat_ref), (index_hbm, index_ref), (length_hbm, length_ref), (init_hbm, init_ref),
        (label_hbm, label_ref), (label_id_hbm, label_id_ref), (count_hbm, count_ref), (neg_id_hbm, neg_id_ref),
        (neg_count_hbm, neg_count_ref), (turn_hbm, turn_ref), (bilinear_hbm, bilinear_ref),
    ]
    late = [
        pltpu.make_async_copy(source, target, load_sem.at[4 + chunks + at])
        for at, (source, target) in enumerate(pairs)
    ]
    for load in early + late:
        load.start()

    y, c, x, z = u // 2, u % 2, p // 4, p % 4
    near_y = [((y + d) % 4) * 2 for d in range(4)]
    near_c = [c, 1 - c]
    near_x = [((x + d) % 4) * 4 for d in range(4)]
    near_z = [(z + d) % 4 for d in range(4)]
    partners = [(near_y[dy] + near_c[dc], near_x[dx] + near_z[dz]) for dy, dc, dx, dz in FARTHEST]
    barrier = pltpu.get_barrier_semaphore()
    for partner in partners[:-1]:
        pl.semaphore_signal(barrier, inc=1, device_id=partner, device_id_type=MESH)

    early[0].wait()
    place = lax.broadcasted_iota(jnp.int32, (cap, items), 1)
    for at in range(devices):
        wanted = jnp.broadcast_to(fetch_ref[:, at : at + 1], (cap, items)) == place
        pick_ref[at * cap : (at + 1) * cap, :] = jnp.where(wanted, 1.0, 0.0).astype(BF16)

    early[1].wait()
    early[2].wait()
    for at in range(chunks):
        early[3 + at].wait()
        cut = slice(at * part, (at + 1) * part)
        hidden_ref[:, cut] = first_layer(feat_ref[...], w_in_ref[:, cut], bias_ref[:, cut])
    early[3 + chunks].wait()
    unit_ref[...] = normalised(jnp.dot(hidden_ref[...], w_out_ref[...], preferred_element_type=F32))
    group = pool_count * cap
    for at in range(user_count):
        rows = slice(at * group, (at + 1) * group)
        outgoing_ref[rows, :] = jnp.dot(pick_ref[rows, :], unit_ref[...], preferred_element_type=F32).astype(BF16)
    pl.semaphore_wait(barrier, devices - 1)

    for turn, (to_user, to_pool) in enumerate(partners[:-1]):
        source = pl.multiple_of((to_user * pool_count + to_pool) * cap, cap)
        pltpu.make_async_remote_copy(
            src_ref=outgoing_ref.at[pl.ds(source, cap)],
            dst_ref=received_ref.at[pl.ds(turn * cap, cap)],
            send_sem=item_send,
            recv_sem=item_recv.at[turn // pool_count],
            device_id=(to_user, to_pool),
            device_id_type=MESH,
        ).start()
    own = pl.multiple_of((u * pool_count + p) * cap, cap)
    keep = pltpu.make_async_copy(
        outgoing_ref.at[pl.ds(own, cap)], received_ref.at[pl.ds((devices - 1) * cap, cap)], item_local
    )
    keep.start()

    def places(slot):
        code = ((y - slot // 512) & 3) * 32 + ((c - slot // 256) & 1) * 16
        code = code + ((x - slot // 64) & 3) * 4 + ((z - slot // 16) & 3)
        rows, events = slot.shape
        table = jnp.broadcast_to(turn_ref[...], (rows, LO))
        turns = [
            jnp.take_along_axis(table, code[:, at : at + LO], axis=1) for at in range(0, events, LO)
        ]
        return jnp.concatenate(turns, axis=1) * cap + slot % cap

    for load in late:
        load.wait()
    lane = lax.broadcasted_iota(jnp.int32, (1, LO), 1)
    ids = jnp.concatenate([label_id_ref[...].astype(F32)] * spread, axis=1)
    id_ref[p] = jnp.broadcast_to(jnp.where(lane // users == p % spread, ids, 0.0), (8, LO))
    info_ref[u] = jnp.concatenate(
        [neg_id_ref[...].astype(F32), jnp.log(neg_count_ref[...].astype(F32)), jnp.zeros((6, LO), F32)], axis=0
    )
    negatives = neg_feat_ref.shape[0]
    hidden_ref[:negatives] = first_layer(neg_feat_ref[...], w_in_ref[...], bias_ref[...])
    neg_ref[u] = normalised(jnp.dot(hidden_ref[:negatives], w_out_ref[...], preferred_element_type=F32))
    place_ref[...] = places(index_ref[...])
    label_wide = jnp.concatenate([label_ref[...]] * spread, axis=1)
    label_place = places(jnp.broadcast_to(label_wide, (8, LO)))[0:1, :users]
    prepare_route(place_ref, length_ref, init_ref, low_ref, high_ref, logit_ref)
    spread_weights(low_ref, high_ref, logit_ref, weight_ref, slot_ref, wide_ref)

    def along_user(ref, send_sem, recv_sem, step):
        return pltpu.make_async_remote_copy(
            src_ref=ref.at[u], dst_ref=ref.at[u], send_sem=send_sem, recv_sem=recv_sem,
            device_id=((u + step) % user_count, p), device_id_type=MESH,
        )

    def along_pool(ref, send_sem, recv_sem, step):
        return pltpu.make_async_remote_copy(
            src_ref=ref.at[p], dst_ref=ref.at[p], send_sem=send_sem, recv_sem=recv_sem,
            device_id=(u, (p + step) % pool_count), device_id_type=MESH,
        )

    def wait_recv(ref, sem):
        pltpu.make_async_remote_copy(
            src_ref=ref, dst_ref=ref, send_sem=sem, recv_sem=sem, device_id=(u, p), device_id_type=MESH
        ).wait_recv()

    def wait_send(ref, sem):
        pltpu.make_async_remote_copy(
            src_ref=ref, dst_ref=ref, send_sem=sem, recv_sem=sem, device_id=(u, p), device_id_type=MESH
        ).wait_send()

    def take(r):
        cut = pl.ds(pl.multiple_of(r * group, group), group)
        here = lax.broadcasted_iota(jnp.int32, (users, group), 1) + r * group
        wanted = jnp.where(here.astype(F32) == label_at, 1.0, 0.0).astype(BF16)
        label_row_ref[...] += jnp.dot(wanted, received_ref[cut, :], preferred_element_type=F32)
        mapped = jnp.dot(received_ref[cut, :], bilinear_ref[...], preferred_element_type=F32)
        mapped_ref[cut, :] = mapped.astype(BF16)
        turned_ref[:, cut] = mapped.T.astype(BF16)
        return jnp.dot(wide_ref[:, cut], mapped_ref[cut, :], preferred_element_type=F32)

    both_ref[...] = jnp.zeros_like(both_ref)
    label_row_ref[...] = jnp.zeros_like(label_row_ref)
    label_at = column(label_place)
    count_log = jnp.log(column(count_ref[...]))

    def take_round(r, carry):
        wait_recv(received_ref.at[pl.ds(pl.multiple_of(r * group, group), group)], item_recv.at[r])
        both_ref[...] += take(r)
        return carry

    lax.fori_loop(0, user_count - 1, take_round, 0)
    keep.wait()
    wait_recv(received_ref.at[pl.ds(0, group - cap)], item_recv.at[user_count - 1])
    both_ref[...] += take(user_count - 1)

    def negative_block(block, to_user, send_sem, recv_sem):
        return pltpu.make_async_remote_copy(
            src_ref=neg_ref.at[block], dst_ref=neg_ref.at[block], send_sem=send_sem, recv_sem=recv_sem,
            device_id=(to_user, p), device_id_type=MESH,
        )

    sibling = y * 2 + near_c[1]
    around = [near_y[step] + c for step in (2, 1, 3)]
    for to_user in around:
        negative_block(u, to_user, neg_send, neg_recv).start()
    negative_block(u, sibling, side_send, side_recv).start()

    def send_info(step, carry):
        along_user(info_ref, info_send, info_recv, step).start()
        return carry

    lax.fori_loop(1, user_count, send_info, 0)

    def send_ids(step, carry):
        along_pool(id_ref, id_send, id_recv, step).start()
        return carry

    lax.fori_loop(1, pool_count, send_ids, 0)

    capsules = squash(both_ref[...])
    for _ in range(1, ITERS):
        add_agreement(capsules, place_ref, turned_ref, score_ref, logit_ref)
        spread_weights(low_ref, high_ref, logit_ref, weight_ref, slot_ref, wide_ref)
        capsules = squash(jnp.dot(wide_ref[...], mapped_ref[...], preferred_element_type=F32))
    user_vec, positive = attend(capsules, label_row_ref[...], count_log)
    vec_ref[p] = user_vec

    row = [(dx, dz) for dx in (2, 1, 3, 0) for dz in (2, 1, 3, 0) if dx or dz]
    for dx, dz in row:
        pltpu.make_async_remote_copy(
            src_ref=vec_ref.at[p], dst_ref=vec_ref.at[p], send_sem=vec_send, recv_sem=vec_recv.at[x],
            device_id=(u, near_x[dx] + near_z[dz]), device_id_type=MESH,
        ).start()
    wait_recv(neg_ref.at[pl.ds(0, len(around))], neg_recv)
    for from_user in around:
        negative_block(from_user, sibling, side_send, side_recv).start()
    for k in range(INTERESTS):
        interest_ref[:, k * width : (k + 1) * width] = capsules[k * users : (k + 1) * users]
    store = pltpu.make_async_copy(interest_ref, interest_hbm, store_sem)
    store.start()
    wait_recv(info_ref.at[pl.ds(0, user_count - 1)], info_recv)
    wait_recv(id_ref.at[pl.ds(0, pool_count - 1)], id_recv)
    wait_recv(neg_ref.at[pl.ds(0, 1 + len(around))], side_recv)
    neg_ids = jnp.concatenate([column(info_ref[at, 0:1, :]) for at in range(user_count)], axis=0)
    neg_logs = jnp.concatenate([column(info_ref[at, 1:2, :]) for at in range(user_count)], axis=0)
    neg_rows = neg_ref[...].reshape(user_count * negatives, width)

    def one_line(line, own_line):
        first = pl.multiple_of(line * spread, spread)
        wait_recv(vec_ref.at[pl.ds(0, spread - 1 if own_line else spread)], vec_recv.at[line])
        vecs = vec_ref[pl.ds(first, spread)].reshape(LO, width)
        line_ids = id_ref[first, 0:1, :]
        for at in range(1, spread):
            line_ids = line_ids + id_ref[first + at, 0:1, :]
        logits = logit_scale * nt_dot(neg_rows, vecs) - neg_logs
        kept = jnp.where(neg_ids != line_ids, jnp.exp(logits), 0.0)
        partial_ref[line] = jnp.broadcast_to(jnp.sum(kept, axis=0, keepdims=True), (8, LO))

    for dx in (2, 1, 3, 0):
        line = near_x[dx] // spread
        one_line(line, dx == 0)
        for dz in (2, 1, 3, 0):
            if dx or dz:
                pltpu.make_async_remote_copy(
                    src_ref=partial_ref.at[line], dst_ref=sum_ref.at[p], send_sem=sum_send, recv_sem=sum_recv,
                    device_id=(u, near_x[dx] + near_z[dz]), device_id_type=MESH,
                ).start()
    sum_ref[p] = partial_ref[x]
    wait_recv(sum_ref.at[pl.ds(0, pool_count - 1)], sum_recv)
    negative = sum_ref[0]
    for at in range(1, pool_count):
        negative = negative + sum_ref[at]
    mine = lax.broadcasted_iota(jnp.int32, (users, LO), 1) == (
        lax.broadcasted_iota(jnp.int32, (users, LO), 0) + (p % spread) * users
    )
    negative = jnp.sum(
        jnp.where(mine, jnp.broadcast_to(negative[0:1], (users, LO)), 0.0), axis=1, keepdims=True
    )
    loss = jnp.log(jnp.exp(positive) + negative) - positive
    eye = lax.broadcasted_iota(jnp.int32, (users, users), 0) == lax.broadcasted_iota(jnp.int32, (users, users), 1)
    loss_ref[...] = jnp.sum(jnp.where(eye, jnp.broadcast_to(loss, (users, users)), 0.0), axis=0, keepdims=True)

    wait_send(outgoing_ref.at[pl.ds(0, (devices - 1) * cap)], item_send)
    wait_send(neg_ref.at[pl.ds(0, len(around))], neg_send)
    wait_send(neg_ref.at[pl.ds(0, 1 + len(around))], side_send)
    store.wait()
    wait_send(info_ref.at[pl.ds(0, user_count - 1)], info_send)
    wait_send(id_ref.at[pl.ds(0, pool_count - 1)], id_send)
    wait_send(vec_ref.at[pl.ds(0, pool_count - 1)], vec_send)
    wait_send(sum_ref.at[pl.ds(0, pool_count - 1)], sum_send)


def hand_out(interest_ref, loss_ref, interest_out, loss_out):
    interest_out[...] = interest_ref[...]
    loss_out[...] = loss_ref[...]


def solution(mesh):
    both = ("user", "pool")
    user_count, pool_count = mesh.shape["user"], mesh.shape["pool"]

    def on_device(
        item_feats, w_in, bias_in, w_out, bilinear, fetch_table, hist_index, hist_len, route_init,
        label_index, label_ids, label_counts, neg_feats, neg_ids, neg_counts,
    ):
        users, events = hist_index.shape
        items, width = item_feats.shape
        hidden = w_in.shape[1]
        devices, _, cap = fetch_table.shape
        slots = devices * cap
        highs = slots // LO
        rows = INTERESTS * users
        negatives = neg_feats.shape[0]
        vmem = pl.BlockSpec(memory_space=pltpu.VMEM)
        hbm = pl.BlockSpec(memory_space=pltpu.HBM)
        dma = pltpu.SemaphoreType.DMA
        operands = (
            item_feats, w_in, bias_in.reshape(1, -1), w_out, bilinear, fetch_table[:, 0, :].T, hist_index,
            hist_len.reshape(1, -1), route_init, label_index.reshape(1, -1), label_ids.reshape(1, -1),
            label_counts.reshape(1, -1), neg_feats, neg_ids.reshape(1, -1), neg_counts.reshape(1, -1),
            jnp.array([TURN], jnp.int32),
        )
        shapes = (
            jax.ShapeDtypeStruct((users, INTERESTS * width), F32),
            jax.ShapeDtypeStruct((1, users), F32),
        )
        results = pl.pallas_call(
            functools.partial(step_kernel, user_count, pool_count),
            out_shape=shapes,
            in_specs=[hbm] * len(operands),
            out_specs=(hbm, pl.BlockSpec(memory_space=pltpu.VMEM)),
            scratch_shapes=[pltpu.VMEM(operand.shape, operand.dtype) for operand in operands] + [
                pltpu.VMEM((slots, items), BF16),
                pltpu.VMEM((items, hidden), BF16),
                pltpu.VMEM((items, width), BF16),
                pltpu.VMEM((slots, width), BF16),
                pltpu.VMEM((slots, width), BF16),
                pltpu.VMEM((slots, width), BF16),
                pltpu.VMEM((width, slots), BF16),
                pltpu.VMEM((users, width), F32),
                pltpu.VMEM((users, events), jnp.int32),
                pltpu.VMEM((users, events, LO), BF16),
                pltpu.VMEM((users, highs, events), F32),
                pltpu.VMEM((INTERESTS + 1, users, events), F32),
                pltpu.VMEM((INTERESTS, users, events), F32),
                pltpu.VMEM((rows * highs, LO), F32),
                pltpu.VMEM((2 * rows, slots), BF16),
                pltpu.VMEM((2 * rows, width), F32),
                pltpu.VMEM((rows, slots), F32),
                pltpu.VMEM((users, INTERESTS * width), F32),
                pltpu.VMEM((user_count, negatives, width), BF16),
                pltpu.VMEM((user_count, 8, LO), F32),
                pltpu.VMEM((pool_count, 8, LO), F32),
                pltpu.VMEM((pool_count, users, width), BF16),
                pltpu.VMEM((pool_count * users // LO, 8, LO), F32),
                pltpu.VMEM((pool_count, 8, LO), F32),
                dma((19,)),
                dma, dma((user_count,)), dma, dma, dma, dma, dma, dma, dma, dma, dma, dma,
                dma, dma((pool_count * users // LO,)), dma, dma,
            ],
            compiler_params=pltpu.CompilerParams(
                collective_id=0, has_side_effects=True, vmem_limit_bytes=60 << 20
            ),
        )(*operands)
        interests, loss = pl.pallas_call(
            hand_out, out_shape=shapes, in_specs=[vmem, vmem], out_specs=(vmem, vmem)
        )(*results)
        return interests, loss.reshape(users)

    in_specs = (
        P(both, None), P(), P(), P(), P(), P(None, both, None), P(both, None), P(both),
        P(both, None, None), P(both), P(both), P(both), P(both, None), P(both), P(both),
    )
    out_specs = (P(both, None), P(both))
    return jax.shard_map(on_device, mesh=mesh, in_specs=in_specs, out_specs=out_specs, check_vma=False)
```

```python
import functools

import jax
import jax.numpy as jnp
from jax import lax
from jax.experimental import pallas as pl
from jax.experimental.pallas import tpu as pltpu
from jax.sharding import PartitionSpec as P

INTERESTS = 4
ITERS = 3
LO = 128

norm_epsilon = 1e-06
attend_scale = 8.0
logit_scale = 20.0

F32 = jnp.float32
BF16 = jnp.bfloat16


MESH = pl.DeviceIdType.MESH


HOPS = (0, 1, 2, 1)
FARTHEST = sorted(
    ((dy, dc, dx, dz) for dy in range(4) for dc in range(2) for dx in range(4) for dz in range(4)),
    key=lambda d: (-HOPS[d[0]] - HOPS[d[2]] - HOPS[d[3]], (d[0] + d[2] + d[3]) % 4, -d[1]),
)
TURN = [0] * len(FARTHEST)
for turn, (dy, dc, dx, dz) in enumerate(FARTHEST):
    TURN[((dy * 2 + dc) * 4 + dx) * 4 + dz] = turn


def normalised(embedding):
    inverse_norm = lax.rsqrt(jnp.sum(embedding * embedding, axis=1, keepdims=True) + norm_epsilon)
    return (embedding * inverse_norm).astype(BF16)


def first_layer(features, w_in, bias):
    hidden = jnp.dot(features, w_in, preferred_element_type=F32) + bias
    return jnp.maximum(hidden, 0.0).astype(BF16)


def nt_dot(a, b):
    return lax.dot_general(a, b, (((1,), (1,)), ((), ())), preferred_element_type=F32)


def column(row):
    size = row.shape[1]
    wide = jnp.broadcast_to(row.astype(F32), (size, size))
    eye = lax.broadcasted_iota(jnp.int32, (size, size), 0) == lax.broadcasted_iota(jnp.int32, (size, size), 1)
    return jnp.sum(jnp.where(eye, wide, 0.0), axis=1, keepdims=True)


def prepare_route(place_ref, length_ref, init_ref, low_ref, high_ref, logit_ref):
    users, events = place_ref.shape
    highs = high_ref.shape[1]
    live = lax.broadcasted_iota(jnp.int32, (users, events), 1).astype(F32) < column(length_ref[...])
    logit_ref[INTERESTS] = jnp.where(live, place_ref[...], -1).astype(F32)
    for k in range(INTERESTS):
        logit_ref[k] = init_ref[:, k, :]

    def one_user(n, carry):
        low = jnp.broadcast_to(place_ref[pl.ds(n, 1), :] & (LO - 1), (LO, events))
        marks = jnp.where(low == lax.broadcasted_iota(jnp.int32, (LO, events), 0), 1.0, 0.0)
        low_ref[n] = marks.T.astype(BF16)
        high = jnp.broadcast_to(logit_ref[INTERESTS, pl.ds(n, 1), :], (highs, events))
        first = (lax.broadcasted_iota(jnp.int32, (highs, events), 0) * LO).astype(F32)
        high_ref[n] = jnp.where((high >= first) & (high < first + LO), 1.0, 0.0)
        return carry

    lax.fori_loop(0, users, one_user, 0, unroll=4)


def spread_weights(low_ref, high_ref, logit_ref, weight_ref, slot_ref, wide_ref):
    _, users, events = weight_ref.shape
    highs = high_ref.shape[1]
    rows = INTERESTS * users
    raised = [jnp.exp(logit_ref[k]) for k in range(INTERESTS)]
    total = raised[0] + raised[1] + raised[2] + raised[3]
    for k in range(INTERESTS):
        weight_ref[k] = (raised[k] / total).astype(BF16).astype(F32)

    def one_user(n, carry):
        mask = high_ref[n]
        spread = [
            (jnp.broadcast_to(weight_ref[k, pl.ds(n, 1), :], (highs, events)) * mask).astype(BF16)
            for k in range(INTERESTS)
        ]
        summed = jnp.dot(jnp.concatenate(spread, axis=0), low_ref[n], preferred_element_type=F32)
        for k in range(INTERESTS):
            slot_ref[pl.ds(pl.multiple_of((k * users + n) * highs, highs), highs), :] = summed[
                k * highs : (k + 1) * highs
            ]
        return carry

    lax.fori_loop(0, users, one_user, 0, unroll=16)
    for high in range(highs):
        part = slot_ref[pl.ds(high, rows, stride=highs), :]
        upper = part.astype(BF16)
        wide_ref[:rows, high * LO : (high + 1) * LO] = upper
        wide_ref[rows:, high * LO : (high + 1) * LO] = (part - upper.astype(F32)).astype(BF16)


def squash(both):
    rows = both.shape[0] // 2
    sums = both[:rows] + both[rows:]
    norm_sq = jnp.sum(sums * sums, axis=1, keepdims=True)
    return sums * jnp.sqrt(norm_sq) / (1.0 + norm_sq)


def add_agreement(capsules, place_ref, turned_ref, score_ref, logit_ref):
    users, events = place_ref.shape
    highs = turned_ref.shape[1] // LO
    score_ref[...] = jnp.dot(capsules.astype(BF16), turned_ref[...], preferred_element_type=F32)
    for group in range(users // 8):
        for chunk in range(events // LO):
            at = place_ref[group * 8 : group * 8 + 8, chunk * LO : (chunk + 1) * LO]
            low = at & (LO - 1)
            block = at >> 7
            found = [jnp.zeros((8, LO), F32)] * INTERESTS
            for high in range(highs):
                here = block == high
                for k in range(INTERESTS):
                    scores = score_ref[
                        k * users + group * 8 : k * users + group * 8 + 8, high * LO : (high + 1) * LO
                    ]
                    picked = jnp.take_along_axis(scores, low, axis=1)
                    found[k] = jnp.where(here, picked, found[k])
            for k in range(INTERESTS):
                logit_ref[k, group * 8 : group * 8 + 8, chunk * LO : (chunk + 1) * LO] += found[k]


def attend(capsules, label_rows):
    users = label_rows.shape[0]
    each = [capsules[k * users : (k + 1) * users] for k in range(INTERESTS)]
    raised = [jnp.exp(attend_scale * jnp.sum(c * label_rows, axis=1, keepdims=True)) for c in each]
    total = raised[0] + raised[1] + raised[2] + raised[3]
    user_vec = (raised[0] / total) * each[0]
    for k in range(1, INTERESTS):
        user_vec = user_vec + (raised[k] / total) * each[k]
    return user_vec.astype(BF16)


def step_kernel(
    user_count, pool_count,
    feat_hbm, w_in_hbm, bias_hbm, w_out_hbm, bilinear_hbm, fetch_hbm, index_hbm, length_hbm, init_hbm,
    label_hbm, label_id_hbm, count_hbm, neg_feat_hbm, neg_id_hbm, neg_count_hbm, turn_hbm,
    interest_hbm, loss_ref,
    feat_ref, w_in_ref, bias_ref, w_out_ref, bilinear_ref, fetch_ref, index_ref, length_ref, init_ref,
    label_ref, label_id_ref, count_ref, neg_feat_ref, neg_id_ref, neg_count_ref, turn_ref, pick_ref, hidden_ref, unit_ref, outgoing_ref, received_ref,
    mapped_ref, turned_ref, label_row_ref, place_ref, low_ref, high_ref, logit_ref, weight_ref, slot_ref, wide_ref, both_ref, score_ref,
    interest_ref, neg_ref, info_ref, id_ref, vec_ref, partial_ref, sum_ref,
    load_sem, item_send, item_recv, item_local, neg_send, neg_recv, side_send, side_recv, store_sem, info_send, info_recv,
    id_send, id_recv, vec_send, vec_recv, sum_send, sum_recv,
):
    u = lax.axis_index("user")
    p = lax.axis_index("pool")
    devices = user_count * pool_count
    cap = fetch_ref.shape[0]
    users, width = vec_ref.shape[1], vec_ref.shape[2]
    items = unit_ref.shape[0]
    hidden = w_in_ref.shape[1]
    chunks = 4
    part = hidden // chunks
    spread = LO // users

    early = [pltpu.make_async_copy(fetch_hbm, fetch_ref, load_sem.at[0])]
    early.append(pltpu.make_async_copy(feat_hbm, feat_ref, load_sem.at[1]))
    early.append(pltpu.make_async_copy(bias_hbm, bias_ref, load_sem.at[2]))
    for at in range(chunks):
        cut = pl.ds(at * part, part)
        early.append(pltpu.make_async_copy(w_in_hbm.at[:, cut], w_in_ref.at[:, cut], load_sem.at[3 + at]))
    early.append(pltpu.make_async_copy(w_out_hbm, w_out_ref, load_sem.at[3 + chunks]))
    pairs = [
        (neg_feat_hbm, neg_feat_ref), (index_hbm, index_ref), (length_hbm, length_ref), (init_hbm, init_ref),
        (label_hbm, label_ref), (label_id_hbm, label_id_ref), (count_hbm, count_ref), (neg_id_hbm, neg_id_ref),
        (neg_count_hbm, neg_count_ref), (turn_hbm, turn_ref), (bilinear_hbm, bilinear_ref),
    ]
    late = [
        pltpu.make_async_copy(source, target, load_sem.at[4 + chunks + at])
        for at, (source, target) in enumerate(pairs)
    ]
    for load in early:
        load.start()

    y, c, x, z = u // 2, u % 2, p // 4, p % 4
    near_y = [((y + d) % 4) * 2 for d in range(4)]
    near_c = [c, 1 - c]
    near_x = [((x + d) % 4) * 4 for d in range(4)]
    near_z = [(z + d) % 4 for d in range(4)]
    partners = [(near_y[dy] + near_c[dc], near_x[dx] + near_z[dz]) for dy, dc, dx, dz in FARTHEST]
    barrier = pltpu.get_barrier_semaphore()
    for partner in partners[:-1]:
        pl.semaphore_signal(barrier, inc=1, device_id=partner, device_id_type=MESH)

    early[0].wait()
    place = lax.broadcasted_iota(jnp.int32, (cap, items), 1)
    for at in range(devices):
        wanted = jnp.broadcast_to(fetch_ref[:, at : at + 1], (cap, items)) == place
        pick_ref[at * cap : (at + 1) * cap, :] = jnp.where(wanted, 1.0, 0.0).astype(BF16)

    early[1].wait()
    early[2].wait()
    for at in range(chunks):
        early[3 + at].wait()
        cut = slice(at * part, (at + 1) * part)
        hidden_ref[:, cut] = first_layer(feat_ref[...], w_in_ref[:, cut], bias_ref[:, cut])
    early[3 + chunks].wait()
    for load in late:
        load.start()
    unit_ref[...] = normalised(jnp.dot(hidden_ref[...], w_out_ref[...], preferred_element_type=F32))
    group = pool_count * cap
    for at in range(user_count):
        rows = slice(at * group, (at + 1) * group)
        outgoing_ref[rows, :] = jnp.dot(pick_ref[rows, :], unit_ref[...], preferred_element_type=F32).astype(BF16)
    pl.semaphore_wait(barrier, devices - 1)

    for turn, (to_user, to_pool) in enumerate(partners[:-1]):
        source = pl.multiple_of((to_user * pool_count + to_pool) * cap, cap)
        pltpu.make_async_remote_copy(
            src_ref=outgoing_ref.at[pl.ds(source, cap)],
            dst_ref=received_ref.at[pl.ds(turn * cap, cap)],
            send_sem=item_send,
            recv_sem=item_recv.at[turn // pool_count],
            device_id=(to_user, to_pool),
            device_id_type=MESH,
        ).start()
    own = pl.multiple_of((u * pool_count + p) * cap, cap)
    keep = pltpu.make_async_copy(
        outgoing_ref.at[pl.ds(own, cap)], received_ref.at[pl.ds((devices - 1) * cap, cap)], item_local
    )
    keep.start()

    def places(slot):
        code = ((y - slot // 512) & 3) * 32 + ((c - slot // 256) & 1) * 16
        code = code + ((x - slot // 64) & 3) * 4 + ((z - slot // 16) & 3)
        rows, events = slot.shape
        table = jnp.broadcast_to(turn_ref[...], (rows, LO))
        turns = [
            jnp.take_along_axis(table, code[:, at : at + LO], axis=1) for at in range(0, events, LO)
        ]
        return jnp.concatenate(turns, axis=1) * cap + slot % cap

    for load in late:
        load.wait()
    lane = lax.broadcasted_iota(jnp.int32, (1, LO), 1)
    ids = jnp.concatenate([label_id_ref[...].astype(F32)] * spread, axis=1)
    id_ref[p] = jnp.broadcast_to(jnp.where(lane // users == p % spread, ids, 0.0), (8, LO))
    info_ref[u] = jnp.concatenate(
        [neg_id_ref[...].astype(F32), jnp.log(neg_count_ref[...].astype(F32)), jnp.zeros((6, LO), F32)], axis=0
    )
    negatives = neg_feat_ref.shape[0]
    hidden_ref[:negatives] = first_layer(neg_feat_ref[...], w_in_ref[...], bias_ref[...])
    neg_ref[u] = normalised(jnp.dot(hidden_ref[:negatives], w_out_ref[...], preferred_element_type=F32))
    place_ref[...] = places(index_ref[...])
    label_wide = jnp.concatenate([label_ref[...]] * spread, axis=1)
    label_place = places(jnp.broadcast_to(label_wide, (8, LO)))[0:1, :users]
    prepare_route(place_ref, length_ref, init_ref, low_ref, high_ref, logit_ref)
    spread_weights(low_ref, high_ref, logit_ref, weight_ref, slot_ref, wide_ref)

    def along_user(ref, send_sem, recv_sem, step):
        return pltpu.make_async_remote_copy(
            src_ref=ref.at[u], dst_ref=ref.at[u], send_sem=send_sem, recv_sem=recv_sem,
            device_id=((u + step) % user_count, p), device_id_type=MESH,
        )

    def along_pool(ref, send_sem, recv_sem, step):
        return pltpu.make_async_remote_copy(
            src_ref=ref.at[p], dst_ref=ref.at[p], send_sem=send_sem, recv_sem=recv_sem,
            device_id=(u, (p + step) % pool_count), device_id_type=MESH,
        )

    def wait_recv(ref, sem):
        pltpu.make_async_remote_copy(
            src_ref=ref, dst_ref=ref, send_sem=sem, recv_sem=sem, device_id=(u, p), device_id_type=MESH
        ).wait_recv()

    def wait_send(ref, sem):
        pltpu.make_async_remote_copy(
            src_ref=ref, dst_ref=ref, send_sem=sem, recv_sem=sem, device_id=(u, p), device_id_type=MESH
        ).wait_send()

    def send_info(step, carry):
        along_user(info_ref, info_send, info_recv, step).start()
        return carry

    lax.fori_loop(1, user_count, send_info, 0)

    def send_ids(step, carry):
        along_pool(id_ref, id_send, id_recv, step).start()
        return carry

    lax.fori_loop(1, pool_count, send_ids, 0)

    def take(r):
        cut = pl.ds(pl.multiple_of(r * group, group), group)
        here = lax.broadcasted_iota(jnp.int32, (users, group), 1) + r * group
        wanted = jnp.where(here.astype(F32) == label_at, 1.0, 0.0).astype(BF16)
        label_row_ref[...] += jnp.dot(wanted, received_ref[cut, :], preferred_element_type=F32)
        mapped = jnp.dot(received_ref[cut, :], bilinear_ref[...], preferred_element_type=F32)
        mapped_ref[cut, :] = mapped.astype(BF16)
        turned_ref[:, cut] = mapped.T.astype(BF16)
        return jnp.dot(wide_ref[:, cut], mapped_ref[cut, :], preferred_element_type=F32)

    both_ref[...] = jnp.zeros_like(both_ref)
    label_row_ref[...] = jnp.zeros_like(label_row_ref)
    label_at = column(label_place)
    count_log = jnp.log(column(count_ref[...]))

    def take_round(r, carry):
        wait_recv(received_ref.at[pl.ds(pl.multiple_of(r * group, group), group)], item_recv.at[r])
        both_ref[...] += take(r)
        return carry

    lax.fori_loop(0, user_count - 1, take_round, 0)
    keep.wait()
    wait_recv(received_ref.at[pl.ds(0, group - cap)], item_recv.at[user_count - 1])
    both_ref[...] += take(user_count - 1)

    def negative_block(block, to_user, send_sem, recv_sem):
        return pltpu.make_async_remote_copy(
            src_ref=neg_ref.at[block], dst_ref=neg_ref.at[block], send_sem=send_sem, recv_sem=recv_sem,
            device_id=(to_user, p), device_id_type=MESH,
        )

    sibling = y * 2 + near_c[1]
    around = [near_y[step] + c for step in (2, 1, 3)]
    for to_user in around:
        negative_block(u, to_user, neg_send, neg_recv).start()
    negative_block(u, sibling, side_send, side_recv).start()

    capsules = squash(both_ref[...])
    for _ in range(1, ITERS):
        add_agreement(capsules, place_ref, turned_ref, score_ref, logit_ref)
        spread_weights(low_ref, high_ref, logit_ref, weight_ref, slot_ref, wide_ref)
        capsules = squash(jnp.dot(wide_ref[...], mapped_ref[...], preferred_element_type=F32))
    user_vec = attend(capsules, label_row_ref[...])
    vec_ref[p] = user_vec

    row = [(dx, dz) for dx in (2, 1, 3, 0) for dz in (2, 1, 3, 0) if dx or dz]
    for dx, dz in row:
        pltpu.make_async_remote_copy(
            src_ref=vec_ref.at[p], dst_ref=vec_ref.at[p], send_sem=vec_send, recv_sem=vec_recv.at[x],
            device_id=(u, near_x[dx] + near_z[dz]), device_id_type=MESH,
        ).start()
    positive = jnp.sum(user_vec.astype(F32) * label_row_ref[...], axis=1, keepdims=True)
    positive = logit_scale * positive - count_log
    wait_recv(neg_ref.at[pl.ds(0, len(around))], neg_recv)
    for from_user in around:
        negative_block(from_user, sibling, side_send, side_recv).start()
    for k in range(INTERESTS):
        interest_ref[:, k * width : (k + 1) * width] = capsules[k * users : (k + 1) * users]
    store = pltpu.make_async_copy(interest_ref, interest_hbm, store_sem)
    store.start()
    wait_recv(info_ref.at[pl.ds(0, user_count - 1)], info_recv)
    wait_recv(id_ref.at[pl.ds(0, pool_count - 1)], id_recv)
    wait_recv(neg_ref.at[pl.ds(0, 1 + len(around))], side_recv)
    neg_ids = jnp.concatenate([column(info_ref[at, 0:1, :]) for at in range(user_count)], axis=0)
    neg_logs = jnp.concatenate([column(info_ref[at, 1:2, :]) for at in range(user_count)], axis=0)
    neg_rows = neg_ref[...].reshape(user_count * negatives, width)

    def one_line(line, own_line):
        first = pl.multiple_of(line * spread, spread)
        wait_recv(vec_ref.at[pl.ds(0, spread - 1 if own_line else spread)], vec_recv.at[line])
        vecs = vec_ref[pl.ds(first, spread)].reshape(LO, width)
        line_ids = id_ref[first, 0:1, :]
        for at in range(1, spread):
            line_ids = line_ids + id_ref[first + at, 0:1, :]
        logits = logit_scale * nt_dot(neg_rows, vecs) - neg_logs
        kept = jnp.where(neg_ids != line_ids, jnp.exp(logits), 0.0)
        partial_ref[line] = jnp.broadcast_to(jnp.sum(kept, axis=0, keepdims=True), (8, LO))

    for dx in (2, 1, 3, 0):
        line = near_x[dx] // spread
        one_line(line, dx == 0)
        for dz in (2, 1, 3, 0):
            if dx or dz:
                pltpu.make_async_remote_copy(
                    src_ref=partial_ref.at[line], dst_ref=sum_ref.at[p], send_sem=sum_send, recv_sem=sum_recv,
                    device_id=(u, near_x[dx] + near_z[dz]), device_id_type=MESH,
                ).start()
    sum_ref[p] = partial_ref[x]
    wait_recv(sum_ref.at[pl.ds(0, pool_count - 1)], sum_recv)
    negative = sum_ref[0]
    for at in range(1, pool_count):
        negative = negative + sum_ref[at]
    mine = lax.broadcasted_iota(jnp.int32, (users, LO), 1) == (
        lax.broadcasted_iota(jnp.int32, (users, LO), 0) + (p % spread) * users
    )
    negative = jnp.sum(
        jnp.where(mine, jnp.broadcast_to(negative[0:1], (users, LO)), 0.0), axis=1, keepdims=True
    )
    loss = jnp.log(jnp.exp(positive) + negative) - positive
    eye = lax.broadcasted_iota(jnp.int32, (users, users), 0) == lax.broadcasted_iota(jnp.int32, (users, users), 1)
    loss_ref[...] = jnp.sum(jnp.where(eye, jnp.broadcast_to(loss, (users, users)), 0.0), axis=0, keepdims=True)

    wait_send(outgoing_ref.at[pl.ds(0, (devices - 1) * cap)], item_send)
    wait_send(neg_ref.at[pl.ds(0, len(around))], neg_send)
    wait_send(neg_ref.at[pl.ds(0, 1 + len(around))], side_send)
    store.wait()
    wait_send(info_ref.at[pl.ds(0, user_count - 1)], info_send)
    wait_send(id_ref.at[pl.ds(0, pool_count - 1)], id_send)
    wait_send(vec_ref.at[pl.ds(0, pool_count - 1)], vec_send)
    wait_send(sum_ref.at[pl.ds(0, pool_count - 1)], sum_send)


def hand_out(interest_ref, loss_ref, interest_out, loss_out):
    interest_out[...] = interest_ref[...]
    loss_out[...] = loss_ref[...]


def solution(mesh):
    both = ("user", "pool")
    user_count, pool_count = mesh.shape["user"], mesh.shape["pool"]

    def on_device(
        item_feats, w_in, bias_in, w_out, bilinear, fetch_table, hist_index, hist_len, route_init,
        label_index, label_ids, label_counts, neg_feats, neg_ids, neg_counts,
    ):
        users, events = hist_index.shape
        items, width = item_feats.shape
        hidden = w_in.shape[1]
        devices, _, cap = fetch_table.shape
        slots = devices * cap
        highs = slots // LO
        rows = INTERESTS * users
        negatives = neg_feats.shape[0]
        vmem = pl.BlockSpec(memory_space=pltpu.VMEM)
        hbm = pl.BlockSpec(memory_space=pltpu.HBM)
        dma = pltpu.SemaphoreType.DMA
        operands = (
            item_feats, w_in, bias_in.reshape(1, -1), w_out, bilinear, fetch_table[:, 0, :].T, hist_index,
            hist_len.reshape(1, -1), route_init, label_index.reshape(1, -1), label_ids.reshape(1, -1),
            label_counts.reshape(1, -1), neg_feats, neg_ids.reshape(1, -1), neg_counts.reshape(1, -1),
            jnp.array([TURN], jnp.int32),
        )
        shapes = (
            jax.ShapeDtypeStruct((users, INTERESTS * width), F32),
            jax.ShapeDtypeStruct((1, users), F32),
        )
        results = pl.pallas_call(
            functools.partial(step_kernel, user_count, pool_count),
            out_shape=shapes,
            in_specs=[hbm] * len(operands),
            out_specs=(hbm, pl.BlockSpec(memory_space=pltpu.VMEM)),
            scratch_shapes=[pltpu.VMEM(operand.shape, operand.dtype) for operand in operands] + [
                pltpu.VMEM((slots, items), BF16),
                pltpu.VMEM((items, hidden), BF16),
                pltpu.VMEM((items, width), BF16),
                pltpu.VMEM((slots, width), BF16),
                pltpu.VMEM((slots, width), BF16),
                pltpu.VMEM((slots, width), BF16),
                pltpu.VMEM((width, slots), BF16),
                pltpu.VMEM((users, width), F32),
                pltpu.VMEM((users, events), jnp.int32),
                pltpu.VMEM((users, events, LO), BF16),
                pltpu.VMEM((users, highs, events), F32),
                pltpu.VMEM((INTERESTS + 1, users, events), F32),
                pltpu.VMEM((INTERESTS, users, events), F32),
                pltpu.VMEM((rows * highs, LO), F32),
                pltpu.VMEM((2 * rows, slots), BF16),
                pltpu.VMEM((2 * rows, width), F32),
                pltpu.VMEM((rows, slots), F32),
                pltpu.VMEM((users, INTERESTS * width), F32),
                pltpu.VMEM((user_count, negatives, width), BF16),
                pltpu.VMEM((user_count, 8, LO), F32),
                pltpu.VMEM((pool_count, 8, LO), F32),
                pltpu.VMEM((pool_count, users, width), BF16),
                pltpu.VMEM((pool_count * users // LO, 8, LO), F32),
                pltpu.VMEM((pool_count, 8, LO), F32),
                dma((19,)),
                dma, dma((user_count,)), dma, dma, dma, dma, dma, dma, dma, dma, dma, dma,
                dma, dma((pool_count * users // LO,)), dma, dma,
            ],
            compiler_params=pltpu.CompilerParams(
                collective_id=0, has_side_effects=True, vmem_limit_bytes=60 << 20
            ),
        )(*operands)
        interests, loss = pl.pallas_call(
            hand_out, grid=(2,), out_shape=shapes,
            in_specs=[pl.BlockSpec((users, 2 * width), lambda i: (0, i)), pl.BlockSpec((1, users), lambda i: (0, 0))],
            out_specs=(
                pl.BlockSpec((users, 2 * width), lambda i: (0, i)), pl.BlockSpec((1, users), lambda i: (0, 0))
            ),
        )(*results)
        return interests, loss.reshape(users)

    in_specs = (
        P(both, None), P(), P(), P(), P(), P(None, both, None), P(both, None), P(both),
        P(both, None, None), P(both), P(both), P(both), P(both, None), P(both), P(both),
    )
    out_specs = (P(both, None), P(both))
    return jax.shard_map(on_device, mesh=mesh, in_specs=in_specs, out_specs=out_specs, check_vma=False)
```
